32 devices in a mesh: gx: 2 (over y), gy: 4 (over z), gz: 4 (over x, core).
Axes of the slice: x: 2, y: 2, z: 4, core: 2. Of those that a mesh axis runs over, the one named last changes fastest.
Arguments:
- positions: float32 [4, 4, 4, 3, 32], P('gx', 'gy', 'gz'), may hold values from 0 to 5, as said below
- counts: int32 [4, 4, 4], P('gx', 'gy', 'gz'), may hold values from 1 to 32, as said below
- scalars: bfloat16 [4, 4, 4, 32, 128], P('gx', 'gy', 'gz'), may hold values from -6 to 6
- vectors: bfloat16 [4, 4, 4, 32, 3, 128], P('gx', 'gy', 'gz'), may hold values from -6 to 6
- radial_in: bfloat16 [2, 8, 64], replicated, may hold values from -2 to 2
- radial_bias: float32 [2, 64], replicated, may hold values from -3 to 3
- radial_out: bfloat16 [2, 64, 512], replicated, may hold values from -0.75 to 0.75
- atom_in: bfloat16 [2, 128, 128], replicated, may hold values from -0.5 to 0.5
- atom_bias: float32 [2, 128], replicated, may hold values from -3 to 3
- atom_out: bfloat16 [2, 128, 512], replicated, may hold values from -0.5 to 0.5
- readout_in: bfloat16 [128, 64], replicated, may hold values from -0.5 to 0.5
- readout_out: float32 [64], replicated, may hold values from -0.75 to 0.75
Outputs:
- scalars_out: bfloat16 [4, 4, 4, 32, 128], P('gx', 'gy', 'gz')
- vectors_out: bfloat16 [4, 4, 4, 32, 3, 128], P('gx', 'gy', 'gz')
- energy: float32 [1], replicated
The draws below stay inside these ranges and needn't reach their ends.
Inputs may be any that keep to these rules, and one draw needn't show every extreme that they name: `counts`: some cell of every draw holds 32 atoms and some other cell one atom. `positions`: the slots of a cell sit on distinct sites of a jittered lattice, so that any two slots, also of neighbouring cells, lie at least 0.5 apart.
All inputs are finite; a program needn't handle non-finite values.
Results may differ from the reference program's by a relative error of at most 0.0075.
Values may be sent and summed in bfloat16 or wider, within the bound.
A program may use at most 64 MiB of HBM per device.

```python
import math
import jax
import jax.numpy as jnp
from jax import lax

CHAN = 128
RADIAL = 64
BASIS = 8
FILTERS = 512
READOUT = 64
SLOTS = 32
LAYERS = 2
NX = 4
NY = 4
NZ = 4


def draw_counts(key, part):
    total = NX * NY * NZ
    key_extra, key_full, key_sparse = jax.random.split(key, 3)
    along = lax.broadcasted_iota(jnp.int32, (NX, NY, NZ), 0)
    level = along * (3 * SLOTS // 4) // NX
    extra = jax.random.randint(key_extra, (NX, NY, NZ), 1, SLOTS // 4 + 1)
    flat = jnp.minimum(level + extra, SLOTS).reshape(total)
    full_cell = jax.random.randint(key_full, (), 0, total)
    sparse_cell = (full_cell + 1 + jax.random.randint(key_sparse, (), 0, total - 1)) % total
    flat = flat.at[full_cell].set(SLOTS).at[sparse_cell].set(1)
    return flat.reshape(NX, NY, NZ).astype(jnp.int32)


def draw_positions(key, part):
    total = NX * NY * NZ
    key_order, key_shift = jax.random.split(key)

    def one_order(one_key):
        return jax.random.permutation(one_key, SLOTS)
    orders = jax.vmap(one_order)(jax.random.split(key_order, total))
    layers_z = SLOTS // 16
    site_x = (orders % 4).astype(jnp.float32)
    site_y = (orders // 4 % 4).astype(jnp.float32)
    site_z = (orders // 16).astype(jnp.float32)
    shift = jax.random.uniform(key_shift, (total, 3, SLOTS), jnp.float32, -0.3, 0.3)
    coords = jnp.stack([(site_x + 0.5 + shift[:, 0]) / 4.0, (site_y + 0.5 + shift[:, 1]) / 4.0, (site_z + 0.5 + shift[:, 2]) / layers_z], axis=1) * 5.0
    return coords.reshape(NX, NY, NZ, 3, SLOTS).astype(jnp.float32)


def level_of(key, shape, cuts, low, largest):
    def one(position, blocks):
        steps = jax.random.uniform(jax.random.fold_in(jax.random.fold_in(key, 6), position), (blocks,), jnp.float32, low / len(cuts), largest / len(cuts))
        return jnp.repeat(jnp.exp(steps), shape[position] // blocks).reshape((-1,) + (1,) * (len(shape) - position - 1))

    level = one(*cuts[0])
    for cut in cuts[1:]:
        level = level * one(*cut)
    return level


def normal_values(own_key, dims, scale, reach, pieces=(), kind=jnp.bfloat16):
    loudness = level_of(own_key, dims, pieces, -0.22, 0.18) if pieces else 1.0
    drawn = jax.random.normal(own_key, dims, jnp.float32) * scale * loudness
    return jnp.minimum(jnp.maximum(drawn, -reach), reach).astype(kind)


def setup_inputs(seed: int = 0) -> dict:
    keys = jax.random.split(jax.random.key(seed), 13)
    positions = draw_positions(jax.random.fold_in(keys[12], 71), 0)
    counts = draw_counts(jax.random.fold_in(keys[12], 71), 0)
    scalars = normal_values(keys[2], (NX, NY, NZ, SLOTS, CHAN), 1.0, 6.0, ((0, 2), (1, 4), (2, 4)))
    vectors = normal_values(keys[3], (NX, NY, NZ, SLOTS, 3, CHAN), 1.0, 6.0, ((0, 2), (1, 4), (2, 4)))
    radial_in = normal_values(keys[4], (LAYERS, BASIS, RADIAL), BASIS ** -0.5, 2.0)
    radial_bias = normal_values(keys[5], (LAYERS, RADIAL), 0.5, 3.0, (), jnp.float32)
    radial_out = normal_values(keys[6], (LAYERS, RADIAL, FILTERS), RADIAL ** -0.5, 0.75)
    atom_in = normal_values(keys[7], (LAYERS, CHAN, CHAN), CHAN ** -0.5, 0.5)
    atom_bias = normal_values(keys[8], (LAYERS, CHAN), 0.5, 3.0, (), jnp.float32)
    atom_out = normal_values(keys[9], (LAYERS, CHAN, FILTERS), CHAN ** -0.5, 0.5)
    readout_in = normal_values(keys[10], (CHAN, READOUT), CHAN ** -0.5, 0.5)
    readout_out = normal_values(keys[11], (READOUT,), READOUT ** -0.5, 0.75, (), jnp.float32)
    return {"positions": positions, "counts": counts, "scalars": scalars, "vectors": vectors, "radial_in": radial_in, "radial_bias": radial_bias, "radial_out": radial_out, "atom_in": atom_in, "atom_bias": atom_bias, "atom_out": atom_out, "readout_in": readout_in, "readout_out": readout_out}


cutoff = 5.0
message_scale = 0.5

def offsets_table():
    index = lax.broadcasted_iota(jnp.int32, (27, 3), 0)
    column = lax.broadcasted_iota(jnp.int32, (27, 3), 1)
    digit = jnp.where(column == 0, index // 9, jnp.where(column == 1, index // 3 % 3, index % 3))
    return (digit - 1).astype(jnp.float32)

def wrap_cells(field):
    widths = ((1, 1), (1, 1), (1, 1)) + ((0, 0),) * (field.ndim - 3)
    return jnp.pad(field, widths, mode='wrap')

def atom_gates(states, atom_in, atom_bias, atom_out):
    lead = states.shape[:-1]
    width = states.shape[-1]
    flat = states.reshape(-1, width)
    hidden = jax.nn.silu(jnp.dot(flat, atom_in, preferred_element_type=jnp.float32) + atom_bias).astype(jnp.bfloat16)
    gates = jnp.dot(hidden, atom_out, preferred_element_type=jnp.float32).astype(jnp.bfloat16)
    return gates.reshape(lead + (4, width))

def receiver_block(start, row_count, near_pos, near_live, own_pos, plain_side, gate_c, pair_g, radial_in, radial_bias, radial_out):
    slots = own_pos.shape[1]
    near_count = near_pos.shape[0]
    width = gate_c.shape[-1]
    mine = lax.dynamic_slice_in_dim(own_pos, start, row_count, 1).T
    displace = near_pos[None, :, :] - mine[:, None, :]
    row_index = start + lax.broadcasted_iota(jnp.int32, (row_count, near_count), 0)
    col_index = lax.broadcasted_iota(jnp.int32, (row_count, near_count), 1)
    itself = (col_index == row_index + 13 * slots).astype(jnp.float32)
    distance = jnp.sqrt(lax.optimization_barrier(jnp.sum(displace * displace, axis=-1)) + itself)
    unit = displace / distance[:, :, None]
    smooth = jnp.where(distance < cutoff, 0.5 * (jnp.cos(math.pi * distance / cutoff) + 1.0), 0.0)
    weight = smooth * near_live[None, :] * (1.0 - itself)
    basis_count = radial_in.shape[0]
    centers = lax.broadcasted_iota(jnp.float32, (basis_count,), 0) * (cutoff / (basis_count - 1))
    sharpness = 0.5 * ((basis_count - 1) / cutoff) ** 2
    basis = jnp.exp(-sharpness * (distance[:, :, None] - centers) ** 2).astype(jnp.bfloat16)
    hidden = jnp.dot(basis.reshape(-1, basis_count), radial_in, preferred_element_type=jnp.float32) + radial_bias
    hidden = jax.nn.silu(hidden).reshape(row_count, near_count, -1) * weight[:, :, None]
    edge = jnp.concatenate([hidden[:, :, None, :], hidden[:, :, None, :] * unit[:, :, :, None]], axis=2).astype(jnp.bfloat16)
    edge_plain = edge[:, :, 0, :].astype(jnp.float32)
    edge_turned = edge[:, :, 1:, :].astype(jnp.float32)
    scalar_part = jnp.einsum('rjh,jc->rhc', edge_plain, plain_side.astype(jnp.float32))
    along_part = jnp.einsum('rjkh,jf->rkhf', edge_turned, gate_c.astype(jnp.float32))
    project_part = jnp.einsum('rjkh,jkf->rhf', edge_turned, pair_g.astype(jnp.float32))
    filters = radial_out.astype(jnp.float32).reshape(-1, 4, width)
    term_a = scalar_part[:, :, :width]
    term_b = scalar_part[:, :, width:].reshape(row_count, -1, 3, width)
    scalar_delta = message_scale * (lax.optimization_barrier(jnp.sum(term_a * filters[None, :, 0, :], axis=1)) + lax.optimization_barrier(jnp.sum(project_part * filters[None, :, 3, :], axis=1)))
    vector_delta = message_scale * (lax.optimization_barrier(jnp.sum(term_b * filters[None, :, None, 1, :], axis=1)) + lax.optimization_barrier(jnp.sum(along_part * filters[None, None, :, 2, :], axis=2)))
    return (scalar_delta, vector_delta)

def cell_update(cell, geo_pad, feat_pad, scalar_state, vector_state, layer_params):
    radial_in, radial_bias, radial_out, atom_in, atom_bias, atom_out = layer_params
    grid_x, grid_y, grid_z, slots, width = scalar_state.shape
    at_x = cell // (grid_y * grid_z)
    at_y = cell // grid_z % grid_y
    at_z = cell % grid_z
    zero = jnp.zeros((), jnp.int32)
    geo_near = lax.dynamic_slice(geo_pad, (at_x, at_y, at_z, zero, zero), (3, 3, 3) + geo_pad.shape[3:]).reshape((27,) + geo_pad.shape[3:])
    feat_near = lax.dynamic_slice(feat_pad, (at_x, at_y, at_z, zero, zero, zero), (3, 3, 3) + feat_pad.shape[3:]).reshape((27 * slots,) + feat_pad.shape[4:])
    own_scalar = lax.dynamic_slice(scalar_state, (at_x, at_y, at_z, zero, zero), (1, 1, 1, slots, width)).reshape(slots, width)
    own_vector = lax.dynamic_slice(vector_state, (at_x, at_y, at_z, zero, zero, zero), (1, 1, 1, slots, 3, width)).reshape(slots, 3, width)
    near_pos = (geo_near[:, :3, :] + offsets_table()[:, :, None] * cutoff).transpose(0, 2, 1).reshape(27 * slots, 3)
    near_live = geo_near[:, 3, :].reshape(27 * slots)
    own_pos = geo_near[13, :3, :]
    own_live = geo_near[13, 3, :]
    gates = atom_gates(feat_near[:, 0, :], atom_in, atom_bias, atom_out)
    near_vectors = feat_near[:, 1:, :].astype(jnp.float32)
    pair_b = (gates[:, 1, None, :].astype(jnp.float32) * near_vectors).astype(jnp.bfloat16)
    pair_g = (gates[:, 3, None, :].astype(jnp.float32) * near_vectors).astype(jnp.bfloat16)
    plain_side = jnp.concatenate([gates[:, 0, :], pair_b.reshape(27 * slots, 3 * width)], axis=1)
    gate_c = gates[:, 2, :]
    row_count = slots // 8

    def one_block(block):
        start = block * row_count
        return receiver_block(start, row_count, near_pos, near_live, own_pos, plain_side, gate_c, pair_g, radial_in, radial_bias, radial_out)
    scalar_delta, vector_delta = lax.map(one_block, jnp.arange(8, dtype=jnp.int32))
    new_scalar = ((own_scalar.astype(jnp.float32) + scalar_delta.reshape(slots, width)) * own_live[:, None]).astype(jnp.bfloat16)
    new_vector = ((own_vector.astype(jnp.float32) + vector_delta.reshape(slots, 3, width)) * own_live[:, None, None]).astype(jnp.bfloat16)
    return (new_scalar, new_vector)

def reference(positions, counts, scalars, vectors, radial_in, radial_bias, radial_out, atom_in, atom_bias, atom_out, readout_in, readout_out):
    live = (lax.broadcasted_iota(jnp.int32, (NX, NY, NZ, SLOTS), 3) < counts[:, :, :, None]).astype(jnp.float32)
    geometry = jnp.concatenate([positions, live[:, :, :, None, :]], axis=3)
    geo_pad = wrap_cells(geometry)
    scalar_state, vector_state = (scalars, vectors)
    for layer in range(LAYERS):
        stacked = jnp.concatenate([scalar_state[:, :, :, :, None, :], vector_state], axis=4)
        feat_pad = wrap_cells(stacked)
        layer_params = (radial_in[layer], radial_bias[layer], radial_out[layer], atom_in[layer], atom_bias[layer], atom_out[layer])

        def one_cell(cell, feat_pad=feat_pad, scalar_state=scalar_state, vector_state=vector_state, layer_params=layer_params):
            return cell_update(cell, geo_pad, feat_pad, scalar_state, vector_state, layer_params)
        new_scalar, new_vector = lax.map(one_cell, jnp.arange(NX * NY * NZ, dtype=jnp.int32))
        scalar_state = new_scalar.reshape(NX, NY, NZ, SLOTS, CHAN)
        vector_state = new_vector.reshape(NX, NY, NZ, SLOTS, 3, CHAN)
    readout_hidden = jax.nn.silu(jnp.dot(scalar_state.reshape(-1, CHAN), readout_in, preferred_element_type=jnp.float32))
    atom_energy = lax.optimization_barrier(jnp.sum(readout_hidden * readout_out, axis=-1)) * live.reshape(-1)
    energy = jnp.sum(atom_energy).reshape(1)
    return (scalar_state, vector_state, energy)
```

```python
import functools
import itertools
import math

import jax
import jax.numpy as jnp
from jax import lax
from jax.experimental import pallas as pl
from jax.experimental.pallas import tpu as pltpu
from jax.sharding import PartitionSpec as P

cutoff = 5.0
message_scale = 0.5
group = 8
chunk = 256

MESH = pl.DeviceIdType.MESH


def beside(axis, step):
    count = lax.axis_size(axis)
    return lax.rem(lax.axis_index(axis) + step + count, count)


def prepare(near_ground, radial_in, radial_bias, tiles, places, counts, radial_block):
    tall, deep, wide = near_ground.shape[:3]
    cells = tall * deep * wide
    slots = places.shape[1]
    rows = near_ground[...].reshape(cells, 128)
    tiles[...] = jnp.zeros(tiles.shape, tiles.dtype)
    tiles[:cells, 0, :] = rows
    for part in range(1, 4):
        tiles[:cells, part, :] = jnp.concatenate(
            [rows[:, part * slots :], rows[:, : part * slots]], axis=1
        )
    lane = lax.broadcasted_iota(jnp.int32, (slots, 8), 1)
    for index, (z, y, x) in enumerate(itertools.product(range(tall), range(deep), range(wide))):
        shift = jnp.where(
            lane == 0, float(x - 1), jnp.where(lane == 1, float(y - 1), float(z - 1))
        )
        places[index, :, :8] = tiles[index].T[:slots, :] + shift * cutoff
    level = tiles[:, 3, :]
    counts[...] = level.T[:1, :].astype(jnp.int32)

    layers, basis_count, hidden_width = radial_in.shape
    box = (group, hidden_width, 128)
    owner = lax.div(lax.broadcasted_iota(jnp.int32, box, 2), basis_count)
    match = owner == lax.broadcasted_iota(jnp.int32, box, 0)
    column = lax.broadcasted_iota(jnp.int32, (hidden_width, 128), 1) - group * basis_count
    for layer in range(layers):
        small = 0.5 * radial_in[layer].astype(jnp.float32)
        tall_form = jnp.concatenate([small] * (128 // basis_count), axis=0)
        wide_form = jnp.concatenate([tall_form] * (128 // hidden_width), axis=1).T[:hidden_width]
        bias = 0.5 * radial_bias[layer : layer + 1, :]
        bias = jnp.concatenate([bias] * (128 // hidden_width), axis=1)
        bias = jnp.broadcast_to(bias, (128, 128)).T[:hidden_width]
        high = bias.astype(jnp.bfloat16).astype(jnp.float32)
        middle = (bias - high).astype(jnp.bfloat16).astype(jnp.float32)
        low = bias - high - middle
        offset = jnp.where(
            column == 0, high, jnp.where(column == 1, middle, jnp.where(column == 2, low, 0.0))
        )
        spread = jnp.where(match, jnp.broadcast_to(wide_form[None], box), 0.0) + offset[None]
        radial_block[layer] = spread.reshape(radial_block.shape[1:]).astype(jnp.bfloat16)


def halo_kernel(first, dims, *refs):
    wide, deep, tall = dims
    if first:
        scalars, vectors, ground, radial_in, radial_bias = refs[:5]
        near, places, counts, radial_block = refs[5:9]
        near_ground, tiles, own_sem, send_sem, recv_sem = refs[9:]
    else:
        block, near, own_sem, send_sem, recv_sem = refs
    sides = [side for side in itertools.product((0, -1, 1), (0, -1, 1)) if side != (0, 0)]
    barrier = pltpu.get_barrier_semaphore()
    for dx, dy in sides:
        pl.semaphore_signal(
            barrier,
            inc=1,
            device_id={"gx": beside("gx", dx), "gy": beside("gy", dy)},
            device_id_type=MESH,
        )
    for dz in (-1, 1):
        pl.semaphore_signal(
            barrier, inc=1, device_id={"gz": beside("gz", dz)}, device_id_type=MESH
        )

    inner = tuple(pl.ds(1, extent) for extent in (tall, deep, wide))
    own = []
    if first:
        own.append(pltpu.make_async_copy(scalars, near.at[inner + (pl.ds(0, 1),)], own_sem.at[0]))
        own.append(pltpu.make_async_copy(vectors, near.at[inner + (pl.ds(1, 3),)], own_sem.at[1]))
        own.append(pltpu.make_async_copy(ground, near_ground.at[inner], own_sem.at[2]))
    else:
        own.append(pltpu.make_async_copy(block, near.at[inner], own_sem.at[0]))
    for copy in own:
        copy.start()
    pl.semaphore_wait(barrier, len(sides) + 2)

    def span(extent, side):
        if side == 0:
            return pl.ds(1, extent), pl.ds(1, extent)
        if side > 0:
            return pl.ds(extent, 1), pl.ds(0, 1)
        return pl.ds(1, 1), pl.ds(extent + 1, 1)

    copies = []

    def send(source, target, device):
        number = len(copies)
        copy = pltpu.make_async_remote_copy(
            src_ref=source,
            dst_ref=target,
            send_sem=send_sem.at[number],
            recv_sem=recv_sem.at[number],
            device_id=device,
            device_id_type=MESH,
        )
        copy.start()
        copies.append(copy)
        return copy

    def inward(at):
        return pl.ds(at.start - 1, at.size)

    def along_plane(dx, dy):
        from_x, to_x = span(wide, dx)
        from_y, to_y = span(deep, dy)
        device = {"gx": beside("gx", dx), "gy": beside("gy", dy)}
        every = pl.ds(1, tall)
        begin = (pl.ds(0, tall), inward(from_y), inward(from_x))
        sent = []
        if first:
            sent.append(send(ground.at[begin], near_ground.at[every, to_y, to_x], device))
            sent.append(
                send(scalars.at[begin], near.at[every, to_y, to_x, pl.ds(0, 1)], device)
            )
            sent.append(
                send(vectors.at[begin], near.at[every, to_y, to_x, pl.ds(1, 3)], device)
            )
        else:
            sent.append(send(block.at[begin], near.at[every, to_y, to_x], device))
        return sent

    def across(dx, dy, whole):
        at_x, at_y = span(wide, dx)[1], span(deep, dy)[1]
        pieces = [near]
        if first:
            pieces = [near_ground, near]
        sent = []
        for dz in (-1, 1):
            from_z, to_z = span(tall, dz)
            device = {"gz": beside("gz", dz)}
            if whole:
                begin = (inward(from_z), pl.ds(0, deep), pl.ds(0, wide))
                if first:
                    sent.append(send(ground.at[begin], near_ground.at[to_z, at_y, at_x], device))
                    sent.append(
                        send(scalars.at[begin], near.at[to_z, at_y, at_x, pl.ds(0, 1)], device)
                    )
                    sent.append(
                        send(vectors.at[begin], near.at[to_z, at_y, at_x, pl.ds(1, 3)], device)
                    )
                else:
                    sent.append(send(block.at[begin], near.at[to_z, at_y, at_x], device))
            else:
                for ref in pieces:
                    sent.append(
                        send(ref.at[from_z, at_y, at_x], ref.at[to_z, at_y, at_x], device)
                    )
        return sent

    order = [(0, -1), (0, 1), (1, 0), (-1, 0), (1, -1), (-1, -1), (1, 1), (-1, 1)]
    direct = {side: along_plane(*side) for side in order[:2]}
    last = [across(0, 0, True)]
    for side in order[2:]:
        direct[side] = along_plane(*side)
    for side in order:
        for copy in direct[side]:
            copy.wait_recv()
        last.append(across(*side, False))
    if first:
        own.pop().wait()
        for sent in last:
            share = len(sent) // 2
            sent[share].wait_recv()
            sent[0].wait_recv()
        prepare(near_ground, radial_in, radial_bias, tiles, places, counts, radial_block)
    for sent in last:
        share = len(sent) // 2
        for place, copy in enumerate(sent):
            if not first or place % share:
                copy.wait_recv()
    for copy in own:
        copy.wait()
    for copy in copies:
        copy.wait_send()


def extended(states, dims, identity, extra=()):
    wide, deep, tall = dims
    slots, width = states[0].shape[-2:]
    vmem = pl.BlockSpec(memory_space=pltpu.VMEM)
    anywhere = pl.BlockSpec(memory_space=pl.ANY)
    outer = (tall + 2, deep + 2, wide + 2)
    cells = math.prod(outer)
    shapes = [jax.ShapeDtypeStruct(outer + (4, slots, width), states[0].dtype)]
    out_specs = [anywhere]
    in_specs = [anywhere] * len(states)
    scratch = []
    pieces = 26
    if extra:
        layers, basis_count, hidden_width = extra[1].shape
        shapes += [
            jax.ShapeDtypeStruct((cells, slots, 128), jnp.float32),
            jax.ShapeDtypeStruct((1, 128), jnp.int32),
            jax.ShapeDtypeStruct((layers, group * hidden_width, 128), jnp.bfloat16),
        ]
        out_specs += [vmem] * 3
        in_specs += [vmem] * 3
        scratch = [
            pltpu.VMEM(outer + (1, 128), jnp.float32),
            pltpu.VMEM((128, 8, 128), jnp.float32),
        ]
        pieces = 8 * 3 + 2 * 3 + 16 * 2
    return pl.pallas_call(
        functools.partial(halo_kernel, bool(extra), dims),
        out_shape=shapes,
        in_specs=in_specs,
        out_specs=out_specs,
        scratch_shapes=scratch
        + [
            pltpu.SemaphoreType.DMA((3,)),
            pltpu.SemaphoreType.DMA((pieces,)),
            pltpu.SemaphoreType.DMA((pieces,)),
        ],
        compiler_params=pltpu.CompilerParams(
            collective_id=identity, has_side_effects=True, vmem_limit_bytes=56 << 20
        ),
        name="halo",
    )(*states, *extra)


def total_kernel(axes, part, out, held, local_sem, send_sem, recv_sem):
    sizes = [lax.axis_size(axis) for axis in axes]
    places = [lax.axis_index(axis) for axis in axes]
    count = math.prod(sizes)
    barrier = pltpu.get_barrier_semaphore()

    def partner(step):
        device = {}
        for axis, size, me in zip(axes, sizes, places):
            device[axis] = lax.rem(me + lax.rem(step, size), size)
            step = lax.div(step, size)
        return device

    def greet(step, carry):
        pl.semaphore_signal(barrier, inc=1, device_id=partner(step), device_id_type=MESH)
        return carry

    lax.fori_loop(1, count, greet, 0)
    own = pltpu.make_async_copy(part, held.at[pl.ds(0, 1)], local_sem)
    own.start()
    pl.semaphore_wait(barrier, count - 1)

    def copy(step):
        return pltpu.make_async_remote_copy(
            src_ref=part,
            dst_ref=held.at[pl.ds(step, 1)],
            send_sem=send_sem.at[step],
            recv_sem=recv_sem.at[step],
            device_id=partner(step),
            device_id_type=MESH,
        )

    def send(step, carry):
        copy(step).start()
        return carry

    def settle(step, carry):
        copy(step).wait()
        return carry

    lax.fori_loop(1, count, send, 0)
    own.wait()
    lax.fori_loop(1, count, settle, 0)
    out[0] = jnp.sum(held[...])


def summed(part, axes, identity):
    count = math.prod(lax.axis_size(axis) for axis in axes)
    vmem = pl.BlockSpec(memory_space=pltpu.VMEM)
    return pl.pallas_call(
        functools.partial(total_kernel, axes),
        out_shape=jax.ShapeDtypeStruct((1,), part.dtype),
        in_specs=[vmem],
        out_specs=pl.BlockSpec(memory_space=pltpu.SMEM),
        scratch_shapes=[
            pltpu.VMEM((count,) + part.shape[1:], part.dtype),
            pltpu.SemaphoreType.DMA,
            pltpu.SemaphoreType.DMA((count,)),
            pltpu.SemaphoreType.DMA((count,)),
        ],
        compiler_params=pltpu.CompilerParams(
            collective_id=identity, has_side_effects=True, vmem_limit_bytes=56 << 20
        ),
        name="total",
    )(part)


def layer_kernel(dims, max_chunks, basis_count, layer, last, *refs):
    counts, places, near, radial_blocks, radial_out_all, atom_in_all = refs[:6]
    atom_bias_all, atom_out_all, readout_in, readout_out = refs[6:10]
    if last:
        scalars_out, vectors_out, part_out = refs[10:13]
    else:
        (block_out,) = refs[10:11]
    fresh, near_place, spots, near_state, edges_even, edges_odd, plain_table, turned_table = refs[-8:]
    wide, deep, tall = dims
    slots, width = near.shape[2:]
    radial_out = radial_out_all.at[layer]
    atom_out = atom_out_all.at[layer]
    hidden_width = radial_out.shape[0]

    inside = [
        (z, y, x)
        for z in range(1, tall + 1)
        for y in range(1, deep + 1)
        for x in range(1, wide + 1)
    ]
    outside = [
        place
        for place in itertools.product(range(tall + 2), range(deep + 2), range(wide + 2))
        if place not in inside
    ]
    total = 0
    starts = []
    for place in inside + outside:
        index = (place[0] * (deep + 2) + place[1]) * (wide + 2) + place[2]
        rows = pl.ds(total, slots)
        near_place[rows, :] = places[index]
        for part in range(4):
            near_state[part, rows, :] = near[index, part].astype(jnp.float32)
        starts.append(total)
        total = total + counts[0, index]
    own_total = starts[len(inside)]
    blank = jnp.zeros((chunk, width), jnp.float32)
    near_place[pl.ds(total, chunk), :] = blank
    for part in range(4):
        near_state[part, pl.ds(total, chunk), :] = blank
    chunks = lax.div(total + chunk - 1, chunk)

    receivers = wide * deep * tall * slots
    quarter = math.pi / cutoff

    @pl.loop(0, chunks)
    def _(step):
        rows = pl.ds(pl.multiple_of(step * chunk, chunk), chunk)
        line = near_place[rows, :].T[:8, :]
        mine = near_place[:receivers, :]
        col = step * chunk + lax.broadcasted_iota(jnp.int32, (receivers, chunk), 1)
        row = lax.broadcasted_iota(jnp.int32, (receivers, chunk), 0)
        unused = jnp.logical_or(col == row, col >= total)
        offset = [line[k : k + 1, :] - mine[:, k : k + 1] for k in range(3)]
        square = offset[0] * offset[0] + offset[1] * offset[1] + offset[2] * offset[2]
        distance = jnp.sqrt(square + jnp.where(unused, 1.0, 0.0))
        inverse = 1.0 / distance
        angle = quarter * distance - 0.5 * math.pi
        turn = angle * angle
        series = 0.0
        for power in (13, 11, 9, 7, 5, 3):
            series = turn * (series + (-1.0) ** (power // 2) / math.factorial(power))
        smooth = 0.5 - 0.5 * (angle + angle * series)
        spots[0, :receivers, rows] = distance
        spots[1, :receivers, rows] = jnp.where(
            jnp.logical_and(distance < cutoff, jnp.logical_not(unused)), smooth, 0.0
        )
        for k in range(3):
            spots[k + 2, :receivers, rows] = offset[k] * inverse
        half = jnp.dot(
            near_state[0, rows, :].astype(jnp.bfloat16),
            (0.5 * atom_in_all[layer].astype(jnp.float32)).astype(jnp.bfloat16),
            preferred_element_type=jnp.float32,
        ) + 0.5 * atom_bias_all[layer : layer + 1, :]
        hidden = (half + half * jnp.tanh(half)).astype(jnp.bfloat16)
        gates = jnp.dot(hidden, atom_out[...], preferred_element_type=jnp.float32).astype(
            jnp.bfloat16
        )
        plain_table[rows, :width] = gates[:, :width]
        gate_b = gates[:, width : 2 * width].astype(jnp.float32)
        gate_c = gates[:, 2 * width : 3 * width]
        gate_g = gates[:, 3 * width :].astype(jnp.float32)
        for part in range(3):
            vector = near_state[part + 1, rows, :]
            plain_table[rows, (part + 1) * width : (part + 2) * width] = (gate_b * vector).astype(
                jnp.bfloat16
            )
            turned_table[part, rows, :width] = gate_c
            turned_table[part, rows, width:] = (gate_g * vector).astype(jnp.bfloat16)

    sharpness = 0.5 * ((basis_count - 1) / cutoff) ** 2
    tile = 16

    def form_edges(first, columns, edges):
        these = pl.ds(first, group)
        centers = lax.broadcasted_iota(jnp.int32, (1, basis_count, chunk), 1).astype(
            jnp.float32
        ) * (cutoff / (basis_count - 1))
        gap = spots[0, these, columns][:, None, :] - centers
        basis = jnp.exp(-sharpness * gap * gap).reshape(group * basis_count, chunk)
        basis = jnp.concatenate(
            [basis, jnp.ones((128 - group * basis_count, chunk), jnp.float32)], axis=0
        )
        half = jnp.dot(
            radial_blocks[layer],
            basis.astype(jnp.bfloat16),
            preferred_element_type=jnp.float32,
        ).reshape(group, hidden_width, chunk)
        active = (half + half * jnp.tanh(half)) * spots[1, these, columns][:, None, :]
        active = active.astype(jnp.bfloat16).reshape(group, hidden_width // tile, tile, chunk)
        edges[0] = active.reshape(group * hidden_width, chunk)
        for k in range(3):
            unit = jnp.broadcast_to(
                spots[k + 2, these, columns][:, None, :], (group, tile, chunk)
            ).astype(jnp.bfloat16)
            edges[k + 1] = (active * unit[:, None]).reshape(group * hidden_width, chunk)

    def contract(first, rows, edges):
        def contracted(left, right, filters):
            product = jnp.dot(left, right, preferred_element_type=jnp.float32)
            product = product.reshape(group, hidden_width, 2 * width)
            return (
                jnp.sum(product[:, :, :width] * filters[0], axis=1),
                jnp.sum(product[:, :, width:] * filters[1], axis=1),
            )

        bank = [
            radial_out[:, part * width : (part + 1) * width].astype(jnp.float32)[None]
            for part in range(4)
        ]
        flat = edges[0]
        scalar, vector0 = contracted(flat, plain_table[rows, : 2 * width], (bank[0], bank[1]))
        vector1, vector2 = contracted(flat, plain_table[rows, 2 * width :], (bank[1], bank[1]))
        vectors = [vector0, vector1, vector2]
        for k in range(3):
            along, project = contracted(
                edges[k + 1], turned_table[k, rows, :], (bank[2], bank[3])
            )
            vectors[k] = vectors[k] + along
            scalar = scalar + project
        for part, change in enumerate([scalar] + vectors):
            fresh[part, pl.ds(first, group), :] += change

    groups = lax.div(own_total + group - 1, group)
    fresh[...] = jnp.zeros(fresh.shape, fresh.dtype)

    def place_of(task):
        turn = lax.div(task, chunks)
        step = task - turn * chunks
        first = pl.multiple_of(turn * group, group)
        return first, pl.ds(pl.multiple_of(step * chunk, chunk), chunk)

    tasks = groups * chunks

    @pl.loop(0, tasks)
    def _(task):
        first, rows = place_of(task)
        form_edges(first, rows, edges_even)
        contract(first, rows, edges_even)
    energy = jnp.zeros((1, 1), jnp.float32)
    for number, (place, start) in enumerate(zip(inside, starts)):
        index = (place[0] * (deep + 2) + place[1]) * (wide + 2) + place[2]
        alive = lax.broadcasted_iota(jnp.int32, (slots, width), 0) < counts[0, index]
        rounded = [
            jnp.where(
                alive,
                near_state[part, pl.ds(start, slots), :]
                + message_scale * fresh[part, pl.ds(start, slots), :],
                0.0,
            ).astype(jnp.bfloat16)
            for part in range(4)
        ]
        if last:
            scalars_out[number] = rounded[0]
            for part in range(3):
                vectors_out[number, part] = rounded[part + 1]
            read = lax.dot_general(
                rounded[0],
                readout_in[...],
                (((1,), (1,)), ((), ())),
                preferred_element_type=jnp.float32,
            )
            read = read / (1.0 + jnp.exp(-read)) * readout_out[...]
            read = jnp.where(alive[:, : read.shape[1]], read, 0.0)
            energy = energy + jnp.sum(read, axis=(0, 1), keepdims=True)
        else:
            for part in range(4):
                block_out[number, part] = rounded[part]
    if last:
        spot = lax.broadcasted_iota(jnp.int32, part_out.shape, 1)
        part_out[...] = jnp.where(spot == 0, jnp.broadcast_to(energy, part_out.shape), 0.0)


def layer_update(layer, dims, basis_count, counts, places, near, params):
    wide, deep, tall = dims
    near = near.reshape((-1,) + near.shape[3:])
    around = near.shape[0]
    slots, width = near.shape[2:]
    hidden_width = params[1].shape[1]
    last = layer == params[1].shape[0] - 1
    cells = wide * deep * tall
    max_chunks = -(-around * slots // chunk)
    span = max_chunks * chunk
    store = around * slots + chunk + slots
    receivers = cells * slots
    vmem = pl.BlockSpec(memory_space=pltpu.VMEM)
    if last:
        shapes = (
            jax.ShapeDtypeStruct((cells, slots, width), jnp.bfloat16),
            jax.ShapeDtypeStruct((cells, 3, slots, width), jnp.bfloat16),
            jax.ShapeDtypeStruct((1, 128), jnp.float32),
        )
    else:
        shapes = (jax.ShapeDtypeStruct((cells, 4, slots, width), jnp.bfloat16),)
    return pl.pallas_call(
        functools.partial(layer_kernel, dims, max_chunks, basis_count, layer, last),
        out_shape=shapes,
        in_specs=[pl.BlockSpec(memory_space=pltpu.SMEM)] + [vmem] * (2 + len(params)),
        out_specs=tuple(vmem for _ in shapes),
        scratch_shapes=[
            pltpu.VMEM((4, receivers + slots, width), jnp.float32),
            pltpu.VMEM((store, width), jnp.float32),
            pltpu.VMEM((5, receivers + 2 * group, span), jnp.float32),
            pltpu.VMEM((4, store, width), jnp.float32),
            pltpu.VMEM((4, group * hidden_width, chunk), jnp.bfloat16),
            pltpu.VMEM((4, group * hidden_width, chunk), jnp.bfloat16),
            pltpu.VMEM((span, 4 * width), jnp.bfloat16),
            pltpu.VMEM((3, span, 2 * width), jnp.bfloat16),
        ],
        compiler_params=pltpu.CompilerParams(vmem_limit_bytes=56 << 20),
        name="message_layer",
    )(counts, places, near, *params)


def on_device(
    positions,
    counts,
    scalars,
    vectors,
    radial_in,
    radial_bias,
    radial_out,
    atom_in,
    atom_bias,
    atom_out,
    readout_in,
    readout_out,
):
    dims = scalars.shape[:3]
    slots, width = scalars.shape[3:]
    level = counts.astype(jnp.float32)[..., None]
    ground = jnp.concatenate([positions.reshape(dims + (3 * slots,)), level], axis=3)
    ground = jnp.pad(ground, ((0, 0),) * 3 + ((0, 128 - ground.shape[3]),))
    ground = ground.transpose(2, 1, 0, 3)[:, :, :, None]
    states = [
        scalars.transpose(2, 1, 0, 3, 4)[:, :, :, None],
        vectors.transpose(2, 1, 0, 4, 3, 5),
    ]
    params = (radial_out, atom_in, atom_bias, atom_out, readout_in.T, readout_out[None, :])
    near, places, near_counts, blocks = extended(states, dims, 0, (ground, radial_in, radial_bias))
    params = (blocks,) + params
    layers = radial_in.shape[0]
    turned = dims[::-1]
    for layer in range(layers):
        made = layer_update(layer, dims, radial_in.shape[1], near_counts, places, near, params)
        if layer < layers - 1:
            (near,) = extended([made[0].reshape(turned + (4, slots, width))], dims, layer + 1)
    new_scalars, new_vectors, part = made
    scalar_state = new_scalars.reshape(turned + (slots, width)).transpose(2, 1, 0, 3, 4)
    vector_state = new_vectors.reshape(turned + (3, slots, width)).transpose(2, 1, 0, 4, 3, 5)
    energy = summed(part, ("gx", "gy", "gz"), layers)
    return (scalar_state, vector_state, energy)


def solution(mesh):
    block = P("gx", "gy", "gz")
    in_specs = (block,) * 4 + (P(),) * 8
    out_specs = (block, block, P())
    return jax.shard_map(
        on_device, mesh=mesh, in_specs=in_specs, out_specs=out_specs, check_vma=False
    )
```

```python
import functools
import itertools
import math

import jax
import jax.numpy as jnp
from jax import lax
from jax.experimental import pallas as pl
from jax.experimental.pallas import tpu as pltpu
from jax.sharding import PartitionSpec as P

cutoff = 5.0
message_scale = 0.5
group = 8
chunk = 512
table_chunk = 256
shares = 4

MESH = pl.DeviceIdType.MESH


def beside(axis, step):
    count = lax.axis_size(axis)
    return lax.rem(lax.axis_index(axis) + step + count, count)


def prepare(near_ground, radial_in, radial_bias, tiles, places, counts, radial_block):
    tall, deep, wide = near_ground.shape[:3]
    cells = tall * deep * wide
    slots = places.shape[1]
    rows = near_ground[...].reshape(cells, 128)
    tiles[...] = jnp.zeros(tiles.shape, tiles.dtype)
    tiles[:cells, 0, :] = rows
    for part in range(1, 4):
        tiles[:cells, part, :] = jnp.concatenate(
            [rows[:, part * slots :], rows[:, : part * slots]], axis=1
        )
    lane = lax.broadcasted_iota(jnp.int32, (slots, 8), 1)
    for index, (z, y, x) in enumerate(itertools.product(range(tall), range(deep), range(wide))):
        shift = jnp.where(
            lane == 0, float(x - 1), jnp.where(lane == 1, float(y - 1), float(z - 1))
        )
        places[index, :, :8] = tiles[index].T[:slots, :] + shift * cutoff
    level = tiles[:, 3, :]
    counts[...] = level.T[:1, :].astype(jnp.int32)

    layers, basis_count, hidden_width = radial_in.shape
    box = (group, hidden_width, 128)
    owner = lax.div(lax.broadcasted_iota(jnp.int32, box, 2), basis_count)
    match = owner == lax.broadcasted_iota(jnp.int32, box, 0)
    column = lax.broadcasted_iota(jnp.int32, (hidden_width, 128), 1) - group * basis_count
    for layer in range(layers):
        small = 0.5 * radial_in[layer].astype(jnp.float32)
        tall_form = jnp.concatenate([small] * (128 // basis_count), axis=0)
        wide_form = jnp.concatenate([tall_form] * (128 // hidden_width), axis=1).T[:hidden_width]
        bias = 0.5 * radial_bias[layer : layer + 1, :]
        bias = jnp.concatenate([bias] * (128 // hidden_width), axis=1)
        bias = jnp.broadcast_to(bias, (128, 128)).T[:hidden_width]
        high = bias.astype(jnp.bfloat16).astype(jnp.float32)
        middle = (bias - high).astype(jnp.bfloat16).astype(jnp.float32)
        low = bias - high - middle
        offset = jnp.where(
            column == 0, high, jnp.where(column == 1, middle, jnp.where(column == 2, low, 0.0))
        )
        spread = jnp.where(match, jnp.broadcast_to(wide_form[None], box), 0.0) + offset[None]
        radial_block[layer] = spread.reshape(radial_block.shape[1:]).astype(jnp.bfloat16)


def halo_kernel(first, dims, *refs):
    wide, deep, tall = dims
    if first:
        level, positions, scalars, vectors, radial_in, radial_bias = refs[:6]
        near, places, counts, radial_block = refs[6:10]
        near_ground, tiles, own_sem, send_sem, recv_sem = refs[10:]
        held = ((scalars, pl.ds(0, 1)), (vectors, pl.ds(1, 3)))
    else:
        block, near, own_sem, send_sem, recv_sem = refs
        held = ((block, pl.ds(0, 4)),)
    barrier = pltpu.get_barrier_semaphore()
    for axis in ("gy", "gx", "gz"):
        for step in (-1, 1):
            pl.semaphore_signal(
                barrier, inc=1, device_id={axis: beside(axis, step)}, device_id_type=MESH
            )
    extents = {"gz": tall, "gy": deep, "gx": wide}
    axes = ("gz", "gy", "gx")
    inner = tuple(pl.ds(1, extents[axis]) for axis in axes)
    own = []
    for place, (state, part) in enumerate(held):
        own.append(
            pltpu.make_async_copy(state, near.at[inner + (part,)], own_sem.at[place])
        )
        own[-1].start()
    if first:
        slots = positions.shape[-1]
        for z, y, x in itertools.product(range(tall), range(deep), range(wide)):
            at = (x * deep + y) * tall + z
            row = [positions[at * 3 + k] for k in range(3)]
            row.append(jnp.full((1, 128 - 3 * slots), level[at], jnp.int32).astype(jnp.float32))
            near_ground[z + 1, y + 1, x + 1] = jnp.concatenate(row, axis=1)
    pl.semaphore_wait(barrier, 6)

    copies = []

    def send(ref, start, axis, step, region):
        extent = extents[axis]
        source, target = (extent, 0) if step > 0 else (1, extent + 1)
        return post(ref, start, axis, step, source, target, region)

    def post(ref, start, axis, step, source, target, region):
        begin, end = dict(region), dict(region)
        begin[axis], end[axis] = pl.ds(source, 1), pl.ds(target, 1)
        begin = [begin[name] for name in axes]
        if start is not None:
            begin = [pl.ds(at.start - 1, at.size) for at in begin]
        number = len(copies)
        copy = pltpu.make_async_remote_copy(
            src_ref=(ref if start is None else start).at[tuple(begin)],
            dst_ref=ref.at[tuple(end[name] for name in axes)],
            send_sem=send_sem.at[number],
            recv_sem=recv_sem.at[number],
            device_id={axis: beside(axis, step)},
            device_id_type=MESH,
        )
        copy.start()
        copies.append(copy)
        return copy

    def both(ref, start, axis, region):
        return [send(ref, start, axis, step, region) for step in (-1, 1)]

    def arrive(sent):
        for copy in sent:
            copy.wait_recv()

    odd = lax.rem(lax.axis_index("gz"), 2)
    own_part = {axis: pl.ds(1, extents[axis]) for axis in axes}
    every = {axis: pl.ds(0, extents[axis] + 2) for axis in axes}
    edge = {axis: {-1: pl.ds(extents[axis] + 1, 1), 1: pl.ds(0, 1)} for axis in axes}
    last = []

    mate = 1 - 2 * odd

    def aside(ref, start, step, region):
        flip = odd if step > 0 else 1 - odd
        source, target = tall + flip * (1 - tall), flip * (tall + 1)
        return post(ref, start, "gz", step * mate, source, target, region)

    def begin(axis, step, out, region):
        if not first:
            return [out(near, block, axis, step, region)]
        return [
            out(near.at[:, :, :, part], state, axis, step, region)
            for state, part in ((vectors, pl.ds(1, 3)), (scalars, pl.ds(0, 1)))
        ]

    def sideways(ref, start, axis, step, region):
        return aside(ref, start, step, region)

    def outward(x, region):
        steps = [step for step, place in ((-1, 1), (1, wide)) if place == x]
        return [(step, send(near, None, "gx", step, region)) for step in steps]

    sides = [(x, step) for x in range(1, wide + 1) for step in (-1, 1)]
    along_y, along_x = {}, {}
    if first:
        ground_y = both(near_ground, None, "gy", own_part)
    for x, step in sides:
        along_y[x, step] = begin("gy", step, send, {**own_part, "gx": pl.ds(x, 1)})
    for step in (-1, 1):
        last += begin("gz", step, sideways, own_part)
    for step in (-1, 1):
        along_x[step] = begin("gx", step, send, own_part)
    if first:
        arrive(ground_y)
        ground_x = both(near_ground, None, "gx", {**own_part, "gy": every["gy"]})
    for step in (-1, 1):
        arrive(along_x[step])
        region = {**own_part, "gx": edge["gx"][step]}
        last += [aside(near, None, -1, region), aside(near, None, 1, region)]
    crossed, turned = {}, []
    for x, step in sides:
        arrive(along_y[x, step])
        region = {**own_part, "gy": edge["gy"][step], "gx": pl.ds(x, 1)}
        crossed[x, step] = aside(near, None, -1, region)
        turned += [(step, *sent) for sent in outward(x, region)]
        last.append(aside(near, None, 1, region))
    if first:
        arrive(ground_x)
        last_ground = both(near_ground, None, "gz", {**every})
    far = pl.ds(odd * (tall + 1), 1)
    for (x, step), copy in crossed.items():
        arrive([copy])
        region = {"gy": edge["gy"][step], "gx": pl.ds(x, 1), "gz": far}
        last += [copy for _, copy in outward(x, region)]
    for step, step_x, copy in turned:
        arrive([copy])
        region = {**own_part, "gy": edge["gy"][step], "gx": edge["gx"][step_x]}
        last.append(aside(near, None, 1, region))
    if first:
        arrive(last_ground)
        prepare(near_ground, radial_in, radial_bias, tiles, places, counts, radial_block)
    for copy in own:
        copy.wait()
    arrive(last)
    for copy in copies:
        copy.wait_send()


def extended(states, dims, identity, extra=()):
    wide, deep, tall = dims
    slots, width = states[0].shape[-2:]
    vmem = pl.BlockSpec(memory_space=pltpu.VMEM)
    anywhere = pl.BlockSpec(memory_space=pl.ANY)
    outer = (tall + 2, deep + 2, wide + 2)
    cells = math.prod(outer)
    shapes = [jax.ShapeDtypeStruct(outer + (4, slots, width), states[0].dtype)]
    out_specs = [anywhere]
    in_specs = [anywhere] * len(states)
    scratch = []
    pieces = 20 + 6 * wide
    if extra:
        layers, basis_count, hidden_width = extra[2].shape
        shapes += [
            jax.ShapeDtypeStruct((cells, slots, 128), jnp.float32),
            jax.ShapeDtypeStruct((1, 128), jnp.int32),
            jax.ShapeDtypeStruct((layers, group * hidden_width, 128), jnp.bfloat16),
        ]
        out_specs += [vmem] * 3
        in_specs = [pl.BlockSpec(memory_space=pltpu.SMEM), vmem] + in_specs + [vmem] * 2
        states = tuple(extra[:2]) + tuple(states) + tuple(extra[2:])
        scratch = [
            pltpu.VMEM(outer + (1, 128), jnp.float32),
            pltpu.VMEM((128, 8, 128), jnp.float32),
        ]
        pieces += 6 + 4 + 2 * wide
    return pl.pallas_call(
        functools.partial(halo_kernel, bool(extra), dims),
        out_shape=shapes,
        in_specs=in_specs,
        out_specs=out_specs,
        scratch_shapes=scratch
        + [
            pltpu.SemaphoreType.DMA((2,)),
            pltpu.SemaphoreType.DMA((pieces,)),
            pltpu.SemaphoreType.DMA((pieces,)),
        ],
        compiler_params=pltpu.CompilerParams(
            collective_id=identity, has_side_effects=True, vmem_limit_bytes=56 << 20
        ),
        name="halo",
    )(*states)


def total_kernel(axes, part, out, held, local_sem, send_sem, recv_sem):
    sizes = [lax.axis_size(axis) for axis in axes]
    partners = []
    for steps in itertools.product(*(range(size) for size in sizes)):
        if any(steps):
            partners.append({axis: beside(axis, step) for axis, step in zip(axes, steps)})
    barrier = pltpu.get_barrier_semaphore()
    for device in partners:
        pl.semaphore_signal(barrier, inc=1, device_id=device, device_id_type=MESH)
    own = pltpu.make_async_copy(part, held.at[pl.ds(0, 1)], local_sem)
    own.start()
    pl.semaphore_wait(barrier, len(partners))
    for place, device in enumerate(partners):
        pltpu.make_async_remote_copy(
            src_ref=part,
            dst_ref=held.at[pl.ds(place + 1, 1)],
            send_sem=send_sem,
            recv_sem=recv_sem,
            device_id=device,
            device_id_type=MESH,
        ).start()
    own.wait()
    rest = held.at[pl.ds(1, len(partners))]
    pltpu.make_async_copy(rest, rest, recv_sem).wait()
    pltpu.make_async_copy(rest, rest, send_sem).wait()
    out[0] = jnp.sum(held[...])


def summed(part, axes, identity):
    count = math.prod(lax.axis_size(axis) for axis in axes)
    vmem = pl.BlockSpec(memory_space=pltpu.VMEM)
    return pl.pallas_call(
        functools.partial(total_kernel, axes),
        out_shape=jax.ShapeDtypeStruct((1,), part.dtype),
        in_specs=[vmem],
        out_specs=pl.BlockSpec(memory_space=pltpu.SMEM),
        scratch_shapes=[
            pltpu.VMEM((count,) + part.shape[1:], part.dtype),
            pltpu.SemaphoreType.DMA,
            pltpu.SemaphoreType.DMA,
            pltpu.SemaphoreType.DMA,
        ],
        compiler_params=pltpu.CompilerParams(
            collective_id=identity, has_side_effects=True, vmem_limit_bytes=56 << 20
        ),
        name="total",
    )(part)


def layer_kernel(dims, basis_count, layer, last, *refs):
    counts, atom_bias_all, readout_in, readout_out = refs[:4]
    fetched = refs[4:10]
    if last:
        scalars_out, vectors_out, part_out = refs[10:13]
    else:
        (block_out,) = refs[10:11]
    places, near, radial_block, radial_out, atom_in, atom_out = refs[-17:-11]
    fresh, near_place, spots, near_state, edges = refs[-11:-6]
    plain_table, turned_table, marks, agenda, slab_sem, fetch_sem = refs[-6:]
    wide, deep, tall = dims
    slots, width = near.shape[4:]
    hidden_width = radial_out.shape[0]

    whole_places, whole_near = fetched[:2]
    fetches = [pltpu.make_async_copy(whole_places, places, fetch_sem.at[0])]
    fetches[0].start()
    slabs = []
    for x in range(wide + 2):
        copy = pltpu.make_async_copy(whole_near.at[:, :, x], near.at[:, :, x], slab_sem.at[x])
        copy.start()
        slabs.append(copy)
    weights = (radial_block, radial_out, atom_in, atom_out)
    for place, (source, target) in enumerate(zip(fetched[2:], weights)):
        copy = pltpu.make_async_copy(source.at[layer], target, fetch_sem.at[place + 1])
        copy.start()
        fetches.append(copy)

    inside = [
        (x, y, z)
        for z in range(1, tall + 1)
        for y in range(1, deep + 1)
        for x in range(1, wide + 1)
    ]
    order = list(itertools.product(range(wide + 2), range(deep + 2), range(tall + 2)))

    def index_of(place):
        x, y, z = place
        return (z * (deep + 2) + y) * (wide + 2) + x

    total = 0
    starts = {}
    bounds = [0]
    fetches[0].wait()
    for place in order:
        starts[place] = total
        near_place[pl.ds(total, slots), :] = places[index_of(place)]
        total = total + counts[0, index_of(place)]
        if place[1:] == (deep + 1, tall + 1):
            bounds.append(total)
    blank = jnp.zeros((table_chunk, width), jnp.float32)
    window = spots.shape[3]
    near_place[pl.ds(total, window), :] = jnp.zeros((window, width), jnp.float32)
    chunks = lax.div(total + table_chunk - 1, table_chunk)
    for number, place in enumerate(inside):
        x = place[0]
        base = lax.div(bounds[x - 1], 16) * 16
        steps = lax.div(bounds[x + 2] - base + chunk - 1, chunk)
        marks[number, 0] = jnp.clip(chunks * table_chunk - steps * chunk, 0, base)
        marks[number, 1] = steps
        marks[number, 2] = starts[place]
        marks[number, 3] = counts[0, index_of(place)]

    for place in order:
        x, y, z = place
        if (y, z) == (0, 0):
            slabs[x].wait()
        for part in range(4):
            near_state[part, pl.ds(starts[place], slots), :] = near[z, y, x, part].astype(
                jnp.float32
            )
    for part in range(4):
        near_state[part, pl.ds(total, table_chunk), :] = blank
    for copy in fetches[1:]:
        copy.wait()

    beyond = pl.ds(pl.multiple_of(chunks * table_chunk, table_chunk), chunk - table_chunk)
    plain_table[beyond, :] = jnp.zeros((chunk - table_chunk, 4 * width), jnp.bfloat16)
    for part in range(3):
        turned_table[part, beyond, :] = jnp.zeros((chunk - table_chunk, 2 * width), jnp.bfloat16)

    @pl.loop(0, chunks)
    def _(step):
        rows = pl.ds(pl.multiple_of(step * table_chunk, table_chunk), table_chunk)
        half = jnp.dot(
            near_state[0, rows, :].astype(jnp.bfloat16),
            (0.5 * atom_in[...].astype(jnp.float32)).astype(jnp.bfloat16),
            preferred_element_type=jnp.float32,
        ) + 0.5 * atom_bias_all[layer : layer + 1, :]
        hidden = (half + half * jnp.tanh(half)).astype(jnp.bfloat16)
        gates = jnp.dot(hidden, atom_out[...], preferred_element_type=jnp.float32).astype(
            jnp.bfloat16
        )
        plain_table[rows, :width] = gates[:, :width]
        gate_b = gates[:, width : 2 * width].astype(jnp.float32)
        gate_c = gates[:, 2 * width : 3 * width]
        gate_g = gates[:, 3 * width :].astype(jnp.float32)
        for part in range(3):
            vector = near_state[part + 1, rows, :]
            plain_table[rows, (part + 1) * width : (part + 2) * width] = (gate_b * vector).astype(
                jnp.bfloat16
            )
            turned_table[part, rows, :width] = gate_c
            turned_table[part, rows, width:] = (gate_g * vector).astype(jnp.bfloat16)

    quarter = math.pi / cutoff
    sharpness = 0.5 * ((basis_count - 1) / cutoff) ** 2
    tile = 16
    fresh[...] = jnp.zeros(fresh.shape, fresh.dtype)

    longest = functools.reduce(jnp.maximum, [marks[number, 1] for number in range(len(inside))])

    @pl.loop(0, longest)
    def _(step):
        columns = pl.ds(pl.multiple_of(step * chunk, chunk), chunk)
        for number in range(len(inside)):
            begin = marks[number, 0] + step * chunk
            start = marks[number, 2]
            line = near_place[pl.ds(begin, chunk), :].T[:8, :]
            mine = near_place[pl.ds(start, slots), :]
            col = begin + lax.broadcasted_iota(jnp.int32, (slots, chunk), 1)
            row = start + lax.broadcasted_iota(jnp.int32, (slots, chunk), 0)
            unused = jnp.logical_or(col == row, col >= total)
            offset = [line[k : k + 1, :] - mine[:, k : k + 1] for k in range(3)]
            square = offset[0] * offset[0] + offset[1] * offset[1] + offset[2] * offset[2]
            square = square + jnp.where(unused, 1.0, 0.0)
            inverse = lax.rsqrt(square)
            distance = square * inverse
            angle = quarter * distance - 0.5 * math.pi
            turn = angle * angle
            series = 0.0
            for power in (13, 11, 9, 7, 5, 3):
                series = turn * (series + (-1.0) ** (power // 2) / math.factorial(power))
            smooth = 0.5 - 0.5 * (angle + angle * series)
            spots[number, 0, :, columns] = distance
            spots[number, 1, :, columns] = jnp.where(
                jnp.logical_and(distance < cutoff, jnp.logical_not(unused)), smooth, 0.0
            )
            for k in range(3):
                spots[number, k + 2, :, columns] = offset[k] * inverse

    tasks = 0
    for number in range(len(inside)):
        steps = marks[number, 1]
        turns = lax.div(marks[number, 3] + group - 1, group)

        @pl.loop(0, turns * steps)
        def _(task, number=number, steps=steps, tasks=tasks):
            turn = lax.div(task, steps)
            agenda[tasks + task, 0] = number
            agenda[tasks + task, 1] = turn * group
            agenda[tasks + task, 2] = task - turn * steps

        tasks = tasks + turns * steps

    share = group // shares

    def spread_basis(task):
        number = agenda[task, 0]
        these = pl.ds(pl.multiple_of(agenda[task, 1], group), group)
        columns = pl.ds(pl.multiple_of(agenda[task, 2] * chunk, chunk), chunk)
        centers = lax.broadcasted_iota(jnp.int32, (1, basis_count, chunk), 1).astype(
            jnp.float32
        ) * (cutoff / (basis_count - 1))
        gap = spots[number, 0, these, columns][:, None, :] - centers
        basis = jnp.exp(-sharpness * gap * gap).reshape(group * basis_count, chunk)
        return jnp.concatenate(
            [basis, jnp.ones((128 - group * basis_count, chunk), jnp.float32)], axis=0
        ).astype(jnp.bfloat16)

    def form_edges(task, basis, part, edges):
        number = agenda[task, 0]
        these = pl.ds(pl.multiple_of(agenda[task, 1], group), group)
        columns = pl.ds(pl.multiple_of(agenda[task, 2] * chunk, chunk), chunk)
        mine = slice(part * share, (part + 1) * share)
        rows = slice(part * share * hidden_width, (part + 1) * share * hidden_width)
        half = jnp.dot(
            radial_block[rows, :], basis, preferred_element_type=jnp.float32
        ).reshape(share, hidden_width, chunk)
        weight = spots[number, 1, these, columns][mine, None, :]
        active = (half + half * jnp.tanh(half)) * weight
        active = active.astype(jnp.bfloat16).reshape(share, hidden_width // tile, tile, chunk)
        edges[0, rows, :] = active.reshape(share * hidden_width, chunk)
        for k in range(3):
            unit = jnp.broadcast_to(
                spots[number, k + 2, these, columns][mine, None, :], (share, tile, chunk)
            ).astype(jnp.bfloat16)
            edges[k + 1, rows, :] = (active * unit[:, None]).reshape(share * hidden_width, chunk)

    def contract(task, edges):
        number = agenda[task, 0]
        these = pl.ds(pl.multiple_of(agenda[task, 1], group), group)
        rows = pl.ds(pl.multiple_of(marks[number, 0] + agenda[task, 2] * chunk, 16), chunk)

        def contracted(left, right, filters):
            product = jnp.dot(left, right, preferred_element_type=jnp.float32)
            product = product.reshape(group, hidden_width, 2 * width)
            return (
                jnp.sum(product[:, :, :width] * filters[0], axis=1),
                jnp.sum(product[:, :, width:] * filters[1], axis=1),
            )

        bank = [
            radial_out[:, part * width : (part + 1) * width].astype(jnp.float32)[None]
            for part in range(4)
        ]
        scalar, vector0 = contracted(edges[0], plain_table[rows, : 2 * width], (bank[0], bank[1]))
        vector1, vector2 = contracted(edges[0], plain_table[rows, 2 * width :], (bank[1], bank[1]))
        vectors = [vector0, vector1, vector2]
        for k in range(3):
            along, project = contracted(edges[k + 1], turned_table[k, rows, :], (bank[2], bank[3]))
            vectors[k] = vectors[k] + along
            scalar = scalar + project
        for part, change in enumerate([scalar] + vectors):
            fresh[number, part, these, :] += change

    @pl.loop(0, tasks)
    def _(task):
        basis = spread_basis(task)
        for part in range(shares):
            form_edges(task, basis, part, edges)
        contract(task, edges)

    energy = jnp.zeros((1, 1), jnp.float32)
    for number, place in enumerate(inside):
        alive = (
            lax.broadcasted_iota(jnp.int32, (slots, width), 0) < counts[0, index_of(place)]
        )
        rounded = [
            jnp.where(
                alive,
                near_state[part, pl.ds(starts[place], slots), :]
                + message_scale * fresh[number, part],
                0.0,
            ).astype(jnp.bfloat16)
            for part in range(4)
        ]
        if last:
            scalars_out[number] = rounded[0]
            for part in range(3):
                vectors_out[number, part] = rounded[part + 1]
            read = lax.dot_general(
                rounded[0],
                readout_in[...],
                (((1,), (1,)), ((), ())),
                preferred_element_type=jnp.float32,
            )
            read = read / (1.0 + jnp.exp(-read)) * readout_out[...]
            read = jnp.where(alive[:, : read.shape[1]], read, 0.0)
            energy = energy + jnp.sum(read, axis=(0, 1), keepdims=True)
        else:
            for part in range(4):
                block_out[number, part] = rounded[part]
    if last:
        spot = lax.broadcasted_iota(jnp.int32, part_out.shape, 1)
        part_out[...] = jnp.where(spot == 0, jnp.broadcast_to(energy, part_out.shape), 0.0)


def layer_update(layer, dims, basis_count, counts, places, near, params):
    wide, deep, tall = dims
    blocks, radial_out, atom_in, atom_bias, atom_out, readout_in, readout_out = params
    around = math.prod(near.shape[:3])
    slots, width = near.shape[4:]
    hidden_width = radial_out.shape[1]
    last = layer == radial_out.shape[0] - 1
    cells = wide * deep * tall
    span = -(-around * slots // table_chunk) * table_chunk + chunk - table_chunk
    window = -(-(3 * (around // (wide + 2)) * slots + 16) // chunk) * chunk
    store = around * slots + window + slots
    vmem = pl.BlockSpec(memory_space=pltpu.VMEM)
    anywhere = pl.BlockSpec(memory_space=pl.ANY)
    if last:
        shapes = (
            jax.ShapeDtypeStruct((cells, slots, width), jnp.bfloat16),
            jax.ShapeDtypeStruct((cells, 3, slots, width), jnp.bfloat16),
            jax.ShapeDtypeStruct((1, 128), jnp.float32),
        )
    else:
        shapes = (jax.ShapeDtypeStruct((cells, 4, slots, width), jnp.bfloat16),)
    fetched = (places, near, blocks, radial_out, atom_in, atom_out)
    return pl.pallas_call(
        functools.partial(layer_kernel, dims, basis_count, layer, last),
        out_shape=shapes,
        in_specs=[pl.BlockSpec(memory_space=pltpu.SMEM)] + [vmem] * 3 + [anywhere] * 6,
        out_specs=tuple(vmem for _ in shapes),
        scratch_shapes=[pltpu.VMEM(array.shape, array.dtype) for array in fetched[:2]]
        + [pltpu.VMEM(array.shape[1:], array.dtype) for array in fetched[2:]]
        + [
            pltpu.VMEM((cells, 4, slots, width), jnp.float32),
            pltpu.VMEM((store, width), jnp.float32),
            pltpu.VMEM((cells, 5, slots, window), jnp.float32),
            pltpu.VMEM((4, store, width), jnp.float32),
            pltpu.VMEM((4, group * hidden_width, chunk), jnp.bfloat16),
            pltpu.VMEM((span, 4 * width), jnp.bfloat16),
            pltpu.VMEM((3, span, 2 * width), jnp.bfloat16),
            pltpu.SMEM((cells, 4), jnp.int32),
            pltpu.SMEM((cells * (slots // group) * (window // chunk), 3), jnp.int32),
            pltpu.SemaphoreType.DMA((wide + 2,)),
            pltpu.SemaphoreType.DMA((5,)),
        ],
        compiler_params=pltpu.CompilerParams(vmem_limit_bytes=56 << 20),
        name="message_layer",
    )(counts, atom_bias, readout_in, readout_out, *fetched)


def on_device(
    positions,
    counts,
    scalars,
    vectors,
    radial_in,
    radial_bias,
    radial_out,
    atom_in,
    atom_bias,
    atom_out,
    readout_in,
    readout_out,
):
    dims = scalars.shape[:3]
    slots, width = scalars.shape[3:]
    level = counts.reshape(-1)
    rows = positions.reshape(-1, 1, slots)
    states = [
        scalars.transpose(2, 1, 0, 3, 4)[:, :, :, None],
        vectors.transpose(2, 1, 0, 4, 3, 5),
    ]
    params = (radial_out, atom_in, atom_bias, atom_out, readout_in.T, readout_out[None, :])
    near, places, near_counts, blocks = extended(
        states, dims, 0, (level, rows, radial_in, radial_bias)
    )
    params = (blocks,) + params
    layers = radial_in.shape[0]
    turned = dims[::-1]
    for layer in range(layers):
        made = layer_update(layer, dims, radial_in.shape[1], near_counts, places, near, params)
        if layer < layers - 1:
            (near,) = extended([made[0].reshape(turned + (4, slots, width))], dims, layer + 1)
    new_scalars, new_vectors, part = made
    scalar_state = new_scalars.reshape(turned + (slots, width)).transpose(2, 1, 0, 3, 4)
    vector_state = new_vectors.reshape(turned + (3, slots, width)).transpose(2, 1, 0, 4, 3, 5)
    energy = summed(part, ("gx", "gy", "gz"), layers)
    return (scalar_state, vector_state, energy)


def solution(mesh):
    block = P("gx", "gy", "gz")
    in_specs = (block,) * 4 + (P(),) * 8
    out_specs = (block, block, P())
    return jax.shard_map(
        on_device, mesh=mesh, in_specs=in_specs, out_specs=out_specs, check_vma=False
    )
```

```python
import functools
import itertools
import math

import jax
import jax.numpy as jnp
from jax import lax
from jax.experimental import pallas as pl
from jax.experimental.pallas import tpu as pltpu
from jax.sharding import PartitionSpec as P

cutoff = 5.0
message_scale = 0.5
group = 8
chunk = 512
table_chunk = 512
shares = 4

MESH = pl.DeviceIdType.MESH


def beside(axis, step):
    count = lax.axis_size(axis)
    return lax.rem(lax.axis_index(axis) + step + count, count)


def prepare(near_ground, radial_in, radial_bias, tiles, counts, radial_block, slots):
    tall, deep, wide = near_ground.shape[:3]
    cells = tall * deep * wide
    rows = near_ground[...].reshape(cells, 128)
    cell = lax.broadcasted_iota(jnp.int32, (cells, 128), 0)
    places = (lax.rem(cell, wide), lax.rem(lax.div(cell, wide), deep), lax.div(cell, wide * deep))
    tiles[...] = jnp.zeros(tiles.shape, tiles.dtype)
    for part in range(3):
        turned = rows
        if part:
            turned = jnp.concatenate([rows[:, part * slots :], rows[:, : part * slots]], axis=1)
        tiles[:, part, :] = turned + (places[part] - 1).astype(jnp.float32) * cutoff
    level = jnp.concatenate([rows[:, 3 * slots :], rows[:, : 3 * slots]], axis=1)
    level = jnp.concatenate([level, jnp.zeros((128 - cells, 128), jnp.float32)], axis=0)
    counts[...] = level.T[:1, :].astype(jnp.int32)

    layers, basis_count, hidden_width = radial_in.shape
    box = (group, hidden_width, 128)
    owner = lax.div(lax.broadcasted_iota(jnp.int32, box, 2), basis_count)
    match = owner == lax.broadcasted_iota(jnp.int32, box, 0)
    column = lax.broadcasted_iota(jnp.int32, (hidden_width, 128), 1) - group * basis_count
    for layer in range(layers):
        small = 0.5 * radial_in[layer].astype(jnp.float32)
        tall_form = jnp.concatenate([small] * (128 // basis_count), axis=0)
        wide_form = jnp.concatenate([tall_form] * (128 // hidden_width), axis=1).T[:hidden_width]
        bias = 0.5 * radial_bias[layer : layer + 1, :]
        bias = jnp.concatenate([bias] * (128 // hidden_width), axis=1)
        bias = jnp.broadcast_to(bias, (128, 128)).T[:hidden_width]
        high = bias.astype(jnp.bfloat16).astype(jnp.float32)
        middle = (bias - high).astype(jnp.bfloat16).astype(jnp.float32)
        low = bias - high - middle
        offset = jnp.where(
            column == 0, high, jnp.where(column == 1, middle, jnp.where(column == 2, low, 0.0))
        )
        spread = jnp.where(match, jnp.broadcast_to(wide_form[None], box), 0.0) + offset[None]
        radial_block[layer] = spread.reshape(radial_block.shape[1:]).astype(jnp.bfloat16)


def halo_kernel(first, dims, *refs):
    wide, deep, tall = dims
    if first:
        scalars, vectors = refs[2:4]
        near = refs[6]
        near_ground = refs[10]
        level, positions, radial_in, radial_bias = refs[11:15]
        results = refs[15:18]
        own_sem, send_sem, recv_sem = refs[18:]
        held = ((scalars, pl.ds(0, 1)), (vectors, pl.ds(1, 3)))
    else:
        block, near, own_sem, send_sem, recv_sem = refs
        held = ((block, pl.ds(0, 4)),)
    barrier = pltpu.get_barrier_semaphore()
    for axis in ("gy", "gx", "gz"):
        for step in (-1, 1):
            pl.semaphore_signal(
                barrier, inc=1, device_id={axis: beside(axis, step)}, device_id_type=MESH
            )
    extents = {"gz": tall, "gy": deep, "gx": wide}
    axes = ("gz", "gy", "gx")
    inner = tuple(pl.ds(1, extents[axis]) for axis in axes)
    own = []
    for place, (state, part) in enumerate(held):
        own.append(
            pltpu.make_async_copy(state, near.at[inner + (part,)], own_sem.at[place])
        )
        own[-1].start()
    if first:
        fetches = []
        sources = refs[:2] + refs[4:6]
        for place, (source, target) in enumerate(zip(sources, refs[11:15])):
            fetches.append(pltpu.make_async_copy(source, target, own_sem.at[2 + place]))
            fetches[-1].start()
        for copy in fetches:
            copy.wait()
        slots = positions.shape[-1]
        for z, y, x in itertools.product(range(tall), range(deep), range(wide)):
            at = (x * deep + y) * tall + z
            row = [positions[at * 3 + k] for k in range(3)]
            row.append(jnp.full((1, 128 - 3 * slots), level[at], jnp.int32).astype(jnp.float32))
            near_ground[z + 1, y + 1, x + 1] = jnp.concatenate(row, axis=1)
    pl.semaphore_wait(barrier, 6)

    copies = []

    def send(ref, start, axis, step, region):
        extent = extents[axis]
        source, target = (extent, 0) if step > 0 else (1, extent + 1)
        return post(ref, start, axis, step, source, target, region)

    def post(ref, start, axis, step, source, target, region):
        begin, end = dict(region), dict(region)
        begin[axis], end[axis] = pl.ds(source, 1), pl.ds(target, 1)
        begin = [begin[name] for name in axes]
        if start is not None:
            begin = [pl.ds(at.start - 1, at.size) for at in begin]
        number = len(copies)
        copy = pltpu.make_async_remote_copy(
            src_ref=(ref if start is None else start).at[tuple(begin)],
            dst_ref=ref.at[tuple(end[name] for name in axes)],
            send_sem=send_sem.at[number],
            recv_sem=recv_sem.at[number],
            device_id={axis: beside(axis, step)},
            device_id_type=MESH,
        )
        copy.start()
        copies.append(copy)
        return copy

    def both(ref, start, axis, region):
        return [send(ref, start, axis, step, region) for step in (-1, 1)]

    def arrive(sent):
        for copy in sent:
            copy.wait_recv()

    odd = lax.rem(lax.axis_index("gz"), 2)
    own_part = {axis: pl.ds(1, extents[axis]) for axis in axes}
    every = {axis: pl.ds(0, extents[axis] + 2) for axis in axes}
    edge = {axis: {-1: pl.ds(extents[axis] + 1, 1), 1: pl.ds(0, 1)} for axis in axes}
    last = []

    mate = 1 - 2 * odd

    def aside(ref, start, step, region):
        flip = odd if step > 0 else 1 - odd
        source, target = tall + flip * (1 - tall), flip * (tall + 1)
        return post(ref, start, "gz", step * mate, source, target, region)

    def begin(axis, step, out, region):
        if not first:
            return [out(near, block, axis, step, region)]
        return [
            out(near.at[:, :, :, part], state, axis, step, region)
            for state, part in ((vectors, pl.ds(1, 3)), (scalars, pl.ds(0, 1)))
        ]

    def sideways(ref, start, axis, step, region):
        return aside(ref, start, step, region)

    def outward(x, region):
        steps = [step for step, place in ((-1, 1), (1, wide)) if place == x]
        return [(step, send(near, None, "gx", step, region)) for step in steps]

    sides = [(x, step) for x in range(1, wide + 1) for step in (-1, 1)]
    along_y, along_x = {}, {}
    if first:
        ground_y = both(near_ground, None, "gy", own_part)
    for x, step in sides:
        along_y[x, step] = begin("gy", step, send, {**own_part, "gx": pl.ds(x, 1)})
    for step in (-1, 1):
        last += begin("gz", step, sideways, own_part)
    for step in (-1, 1):
        along_x[step] = begin("gx", step, send, own_part)
    if first:
        arrive(ground_y)
        ground_x = both(near_ground, None, "gx", {**own_part, "gy": every["gy"]})
    for step in (-1, 1):
        arrive(along_x[step])
        region = {**own_part, "gx": edge["gx"][step]}
        last += [aside(near, None, -1, region), aside(near, None, 1, region)]
    crossed, turned = {}, []
    for x, step in sides:
        arrive(along_y[x, step])
        region = {**own_part, "gy": edge["gy"][step], "gx": pl.ds(x, 1)}
        crossed[x, step] = aside(near, None, -1, region)
        turned += [(step, *sent) for sent in outward(x, region)]
        last.append(aside(near, None, 1, region))
    if first:
        arrive(ground_x)
        last_ground = both(near_ground, None, "gz", {**every})
    far = pl.ds(odd * (tall + 1), 1)
    for (x, step), copy in crossed.items():
        arrive([copy])
        region = {"gy": edge["gy"][step], "gx": pl.ds(x, 1), "gz": far}
        last += [copy for _, copy in outward(x, region)]
    for step, step_x, copy in turned:
        arrive([copy])
        region = {**own_part, "gy": edge["gy"][step], "gx": edge["gx"][step_x]}
        last.append(aside(near, None, 1, region))
    if first:
        arrive(last_ground)
        prepare(near_ground, radial_in, radial_bias, *results, slots)
        for place, (source, target) in enumerate(zip(results, refs[7:10])):
            own.append(pltpu.make_async_copy(source, target, own_sem.at[6 + place]))
            own[-1].start()
    for copy in own:
        copy.wait()
    arrive(last)
    for copy in copies:
        copy.wait_send()


def extended(states, dims, identity, extra=()):
    wide, deep, tall = dims
    slots, width = states[0].shape[-2:]
    anywhere = pl.BlockSpec(memory_space=pl.ANY)
    outer = (tall + 2, deep + 2, wide + 2)
    cells = math.prod(outer)
    shapes = [jax.ShapeDtypeStruct(outer + (4, slots, width), states[0].dtype)]
    scratch = []
    pieces = 20 + 6 * wide
    if extra:
        layers, basis_count, hidden_width = extra[2].shape
        shapes += [
            jax.ShapeDtypeStruct((cells, 8, 128), jnp.float32),
            jax.ShapeDtypeStruct((1, 128), jnp.int32),
            jax.ShapeDtypeStruct((layers, group * hidden_width, 128), jnp.bfloat16),
        ]
        states = tuple(extra[:2]) + tuple(states) + tuple(extra[2:])
        scratch = [pltpu.VMEM(outer + (1, 128), jnp.float32)]
        scratch.append(pltpu.SMEM(extra[0].shape, extra[0].dtype))
        scratch += [pltpu.VMEM(array.shape, array.dtype) for array in extra[1:]]
        scratch += [pltpu.VMEM(shape.shape, shape.dtype) for shape in shapes[1:]]
        pieces += 6 + 4 + 2 * wide
    return pl.pallas_call(
        functools.partial(halo_kernel, bool(extra), dims),
        out_shape=shapes,
        in_specs=[anywhere] * len(states),
        out_specs=[anywhere] * len(shapes),
        scratch_shapes=scratch
        + [
            pltpu.SemaphoreType.DMA((9,)),
            pltpu.SemaphoreType.DMA((pieces,)),
            pltpu.SemaphoreType.DMA((pieces,)),
        ],
        compiler_params=pltpu.CompilerParams(
            collective_id=identity, has_side_effects=True, vmem_limit_bytes=56 << 20
        ),
        name="halo",
    )(*states)


def total_kernel(axes, part, out, held, local_sem, send_sem, recv_sem):
    sizes = [lax.axis_size(axis) for axis in axes]
    partners = []
    order = sorted(
        itertools.product(*(range(size) for size in sizes)),
        key=lambda steps: -sum(min(step, size - step) for step, size in zip(steps, sizes)),
    )
    for steps in order:
        if any(steps):
            partners.append({axis: beside(axis, step) for axis, step in zip(axes, steps)})
    barrier = pltpu.get_barrier_semaphore()
    for device in partners:
        pl.semaphore_signal(barrier, inc=1, device_id=device, device_id_type=MESH)
    own = pltpu.make_async_copy(part, held.at[pl.ds(0, 1)], local_sem)
    own.start()
    pl.semaphore_wait(barrier, len(partners))
    for place, device in enumerate(partners):
        pltpu.make_async_remote_copy(
            src_ref=part,
            dst_ref=held.at[pl.ds(place + 1, 1)],
            send_sem=send_sem,
            recv_sem=recv_sem,
            device_id=device,
            device_id_type=MESH,
        ).start()
    own.wait()
    rest = held.at[pl.ds(1, len(partners))]
    pltpu.make_async_copy(rest, rest, recv_sem).wait()
    pltpu.make_async_copy(rest, rest, send_sem).wait()
    out[0] = jnp.sum(held[...])


def summed(part, axes, identity):
    count = math.prod(lax.axis_size(axis) for axis in axes)
    return pl.pallas_call(
        functools.partial(total_kernel, axes),
        out_shape=jax.ShapeDtypeStruct((1,), part.dtype),
        in_specs=[pl.BlockSpec(memory_space=pl.ANY)],
        out_specs=pl.BlockSpec(memory_space=pltpu.SMEM),
        scratch_shapes=[
            pltpu.VMEM((count,) + part.shape[1:], part.dtype),
            pltpu.SemaphoreType.DMA,
            pltpu.SemaphoreType.DMA,
            pltpu.SemaphoreType.DMA,
        ],
        compiler_params=pltpu.CompilerParams(
            collective_id=identity, has_side_effects=True, vmem_limit_bytes=56 << 20
        ),
        name="total",
    )(part)


def layer_kernel(dims, basis_count, layer, last, *refs):
    fetched = refs[:10]
    if last:
        scalars_out, vectors_out, part_out = refs[10:13]
    else:
        (block_out,) = refs[10:11]
    counts, tiles, near, radial_block, radial_out, atom_in, atom_out = refs[-21:-14]
    atom_bias_all, readout_in, readout_out = refs[-14:-11]
    fresh, near_place, spots, near_state, edges = refs[-11:-6]
    plain_table, turned_table, marks, agenda, slab_sem, fetch_sem = refs[-6:]
    wide, deep, tall = dims
    slots, width = near.shape[4:]
    hidden_width = radial_out.shape[0]

    whole_near = fetched[2]
    slabs, fetches = [], []
    for place, target in enumerate((counts, tiles)):
        fetches.append(pltpu.make_async_copy(fetched[place], target, fetch_sem.at[place]))
        fetches[-1].start()
    for x in range(wide + 2):
        copy = pltpu.make_async_copy(whole_near.at[:, :, x], near.at[:, :, x], slab_sem.at[x])
        copy.start()
        slabs.append(copy)
    weights = (radial_block, radial_out, atom_in, atom_out, atom_bias_all, readout_in, readout_out)
    for place, (source, target) in enumerate(zip(fetched[3:], weights)):
        if place < 4:
            source = source.at[layer]
        copy = pltpu.make_async_copy(source, target, fetch_sem.at[place + 2])
        copy.start()
        fetches.append(copy)

    inside = [
        (x, y, z)
        for z in range(1, tall + 1)
        for y in range(1, deep + 1)
        for x in range(1, wide + 1)
    ]
    order = list(itertools.product(range(wide + 2), range(deep + 2), range(tall + 2)))

    def index_of(place):
        x, y, z = place
        return (z * (deep + 2) + y) * (wide + 2) + x

    total = 0
    starts = {}
    bounds = [0]
    for copy in fetches[:2]:
        copy.wait()
    for place in order:
        starts[place] = total
        near_place[pl.ds(total, slots), :8] = tiles[index_of(place)].T[:slots, :]
        total = total + counts[0, index_of(place)]
        if place[1:] == (deep + 1, tall + 1):
            bounds.append(total)
    blank = jnp.zeros((table_chunk, width), jnp.float32)
    window = spots.shape[3]
    near_place[pl.ds(total, window), :] = jnp.zeros((window, width), jnp.float32)
    chunks = lax.div(total + table_chunk - 1, table_chunk)
    for number, place in enumerate(inside):
        x = place[0]
        base = lax.div(bounds[x - 1], 16) * 16
        steps = lax.div(bounds[x + 2] - base + chunk - 1, chunk)
        marks[number, 0] = jnp.clip(chunks * table_chunk - steps * chunk, 0, base)
        marks[number, 1] = steps
        marks[number, 2] = starts[place]
        marks[number, 3] = counts[0, index_of(place)]

    quarter = math.pi / cutoff
    sharpness = 0.5 * ((basis_count - 1) / cutoff) ** 2
    tile = 16
    fresh[...] = jnp.zeros(fresh.shape, fresh.dtype)

    longest = functools.reduce(jnp.maximum, [marks[number, 1] for number in range(len(inside))])

    @pl.loop(0, longest)
    def _(step):
        columns = pl.ds(pl.multiple_of(step * chunk, chunk), chunk)
        for number in range(len(inside)):
            begin = marks[number, 0] + step * chunk
            start = marks[number, 2]
            line = near_place[pl.ds(begin, chunk), :].T[:8, :]
            mine = near_place[pl.ds(start, slots), :]
            col = begin + lax.broadcasted_iota(jnp.int32, (slots, chunk), 1)
            row = start + lax.broadcasted_iota(jnp.int32, (slots, chunk), 0)
            unused = jnp.logical_or(col == row, col >= total)
            offset = [line[k : k + 1, :] - mine[:, k : k + 1] for k in range(3)]
            square = offset[0] * offset[0] + offset[1] * offset[1] + offset[2] * offset[2]
            square = square + jnp.where(unused, 1.0, 0.0)
            inverse = lax.rsqrt(square)
            distance = square * inverse
            angle = quarter * distance - 0.5 * math.pi
            turn = angle * angle
            series = 0.0
            for power in (13, 11, 9, 7, 5, 3):
                series = turn * (series + (-1.0) ** (power // 2) / math.factorial(power))
            smooth = 0.5 - 0.5 * (angle + angle * series)
            spots[number, 0, :, columns] = distance
            spots[number, 1, :, columns] = jnp.where(
                jnp.logical_and(distance < cutoff, jnp.logical_not(unused)), smooth, 0.0
            )
            for k in range(3):
                spots[number, k + 2, :, columns] = offset[k] * inverse

    for place in order:
        x, y, z = place
        if (y, z) == (0, 0):
            slabs[x].wait()
        for part in range(4):
            near_state[part, pl.ds(starts[place], slots), :] = near[z, y, x, part].astype(
                jnp.float32
            )
    for part in range(4):
        near_state[part, pl.ds(total, table_chunk), :] = blank
    for copy in fetches[2:]:
        copy.wait()

    @pl.loop(0, chunks)
    def _(step):
        rows = pl.ds(pl.multiple_of(step * table_chunk, table_chunk), table_chunk)
        half = jnp.dot(
            near_state[0, rows, :].astype(jnp.bfloat16),
            (0.5 * atom_in[...].astype(jnp.float32)).astype(jnp.bfloat16),
            preferred_element_type=jnp.float32,
        ) + 0.5 * atom_bias_all[layer : layer + 1, :]
        hidden = (half + half * jnp.tanh(half)).astype(jnp.bfloat16)
        gates = jnp.dot(hidden, atom_out[...], preferred_element_type=jnp.float32).astype(
            jnp.bfloat16
        )
        plain_table[rows, :width] = gates[:, :width]
        gate_b = gates[:, width : 2 * width].astype(jnp.float32)
        gate_c = gates[:, 2 * width : 3 * width]
        gate_g = gates[:, 3 * width :].astype(jnp.float32)
        for part in range(3):
            vector = near_state[part + 1, rows, :]
            plain_table[rows, (part + 1) * width : (part + 2) * width] = (gate_b * vector).astype(
                jnp.bfloat16
            )
            turned_table[part, rows, :width] = gate_c
            turned_table[part, rows, width:] = (gate_g * vector).astype(jnp.bfloat16)

    tasks = 0
    for number in range(len(inside)):
        steps = marks[number, 1]
        turns = lax.div(marks[number, 3] + group - 1, group)

        @pl.loop(0, turns * steps)
        def _(task, number=number, steps=steps, tasks=tasks):
            turn = lax.div(task, steps)
            agenda[tasks + task, 0] = number
            agenda[tasks + task, 1] = turn * group
            agenda[tasks + task, 2] = task - turn * steps

        tasks = tasks + turns * steps

    share = group // shares

    def spread_basis(task):
        number = agenda[task, 0]
        these = pl.ds(pl.multiple_of(agenda[task, 1], group), group)
        columns = pl.ds(pl.multiple_of(agenda[task, 2] * chunk, chunk), chunk)
        centers = lax.broadcasted_iota(jnp.int32, (1, basis_count, chunk), 1).astype(
            jnp.float32
        ) * (cutoff / (basis_count - 1))
        gap = spots[number, 0, these, columns][:, None, :] - centers
        basis = jnp.exp(-sharpness * gap * gap).reshape(group * basis_count, chunk)
        return jnp.concatenate(
            [basis, jnp.ones((128 - group * basis_count, chunk), jnp.float32)], axis=0
        ).astype(jnp.bfloat16)

    def form_edges(task, basis, part, edges):
        number = agenda[task, 0]
        these = pl.ds(pl.multiple_of(agenda[task, 1], group), group)
        columns = pl.ds(pl.multiple_of(agenda[task, 2] * chunk, chunk), chunk)
        mine = slice(part * share, (part + 1) * share)
        rows = slice(part * share * hidden_width, (part + 1) * share * hidden_width)
        half = jnp.dot(
            radial_block[rows, :], basis, preferred_element_type=jnp.float32
        ).reshape(share, hidden_width, chunk)
        weight = spots[number, 1, these, columns][mine, None, :]
        active = (half + half * jnp.tanh(half)) * weight
        active = active.astype(jnp.bfloat16).reshape(share, hidden_width // tile, tile, chunk)
        edges[0, rows, :] = active.reshape(share * hidden_width, chunk)
        for k in range(3):
            unit = jnp.broadcast_to(
                spots[number, k + 2, these, columns][mine, None, :], (share, tile, chunk)
            ).astype(jnp.bfloat16)
            edges[k + 1, rows, :] = (active * unit[:, None]).reshape(share * hidden_width, chunk)

    def contract(task, edges):
        number = agenda[task, 0]
        these = pl.ds(pl.multiple_of(agenda[task, 1], group), group)
        rows = pl.ds(pl.multiple_of(marks[number, 0] + agenda[task, 2] * chunk, 16), chunk)

        def contracted(left, right, filters):
            product = jnp.dot(left, right, preferred_element_type=jnp.float32)
            product = product.reshape(group, hidden_width, 2 * width)
            return (
                jnp.sum(product[:, :, :width] * filters[0], axis=1),
                jnp.sum(product[:, :, width:] * filters[1], axis=1),
            )

        bank = [
            radial_out[:, part * width : (part + 1) * width].astype(jnp.float32)[None]
            for part in range(4)
        ]
        scalar, vector0 = contracted(edges[0], plain_table[rows, : 2 * width], (bank[0], bank[1]))
        vector1, vector2 = contracted(edges[0], plain_table[rows, 2 * width :], (bank[1], bank[1]))
        vectors = [vector0, vector1, vector2]
        for k in range(3):
            along, project = contracted(edges[k + 1], turned_table[k, rows, :], (bank[2], bank[3]))
            vectors[k] = vectors[k] + along
            scalar = scalar + project
        for part, change in enumerate([scalar] + vectors):
            fresh[number, part, these, :] += change

    @pl.loop(0, tasks)
    def _(task):
        basis = spread_basis(task)
        for part in range(shares):
            form_edges(task, basis, part, edges)
        contract(task, edges)

    energy = jnp.zeros((1, 1), jnp.float32)
    for number, place in enumerate(inside):
        alive = (
            lax.broadcasted_iota(jnp.int32, (slots, width), 0) < counts[0, index_of(place)]
        )
        rounded = [
            jnp.where(
                alive,
                near_state[part, pl.ds(starts[place], slots), :]
                + message_scale * fresh[number, part],
                0.0,
            ).astype(jnp.bfloat16)
            for part in range(4)
        ]
        if last:
            scalars_out[number] = rounded[0]
            for part in range(3):
                vectors_out[number, part] = rounded[part + 1]
            read = lax.dot_general(
                rounded[0],
                readout_in[...],
                (((1,), (1,)), ((), ())),
                preferred_element_type=jnp.float32,
            )
            read = read / (1.0 + jnp.exp(-read)) * readout_out[...]
            read = jnp.where(alive[:, : read.shape[1]], read, 0.0)
            energy = energy + jnp.sum(read, axis=(0, 1), keepdims=True)
        else:
            for part in range(4):
                block_out[number, part] = rounded[part]
    if last:
        spot = lax.broadcasted_iota(jnp.int32, part_out.shape, 1)
        part_out[...] = jnp.where(spot == 0, jnp.broadcast_to(energy, part_out.shape), 0.0)


def layer_update(layer, dims, basis_count, counts, tiles, near, params):
    wide, deep, tall = dims
    radial_out = params[1]
    around = math.prod(near.shape[:3])
    slots, width = near.shape[4:]
    hidden_width = radial_out.shape[1]
    last = layer == radial_out.shape[0] - 1
    cells = wide * deep * tall
    span = -(-around * slots // table_chunk) * table_chunk + chunk - table_chunk
    window = -(-(3 * (around // (wide + 2)) * slots + 16) // chunk) * chunk
    store = around * slots + window + slots
    vmem = pl.BlockSpec(memory_space=pltpu.VMEM)
    anywhere = pl.BlockSpec(memory_space=pl.ANY)
    if last:
        shapes = (
            jax.ShapeDtypeStruct((cells, slots, width), jnp.bfloat16),
            jax.ShapeDtypeStruct((cells, 3, slots, width), jnp.bfloat16),
            jax.ShapeDtypeStruct((1, 128), jnp.float32),
        )
    else:
        shapes = (jax.ShapeDtypeStruct((cells, 4, slots, width), jnp.bfloat16),)
    fetched = (counts, tiles, near) + params
    return pl.pallas_call(
        functools.partial(layer_kernel, dims, basis_count, layer, last),
        out_shape=shapes,
        in_specs=[anywhere] * len(fetched),
        out_specs=tuple(vmem for _ in shapes),
        scratch_shapes=[pltpu.SMEM(counts.shape, counts.dtype)]
        + [pltpu.VMEM(array.shape, array.dtype) for array in fetched[1:3]]
        + [pltpu.VMEM(array.shape[1:], array.dtype) for array in params[:4]]
        + [pltpu.VMEM(array.shape, array.dtype) for array in params[4:]]
        + [
            pltpu.VMEM((cells, 4, slots, width), jnp.float32),
            pltpu.VMEM((store, width), jnp.float32),
            pltpu.VMEM((cells, 5, slots, window), jnp.float32),
            pltpu.VMEM((4, store, width), jnp.float32),
            pltpu.VMEM((4, group * hidden_width, chunk), jnp.bfloat16),
            pltpu.VMEM((span, 4 * width), jnp.bfloat16),
            pltpu.VMEM((3, span, 2 * width), jnp.bfloat16),
            pltpu.SMEM((cells, 4), jnp.int32),
            pltpu.SMEM((cells * (slots // group) * (window // chunk), 3), jnp.int32),
            pltpu.SemaphoreType.DMA((wide + 2,)),
            pltpu.SemaphoreType.DMA((9,)),
        ],
        compiler_params=pltpu.CompilerParams(vmem_limit_bytes=56 << 20),
        name="message_layer",
    )(*fetched)


def on_device(
    positions,
    counts,
    scalars,
    vectors,
    radial_in,
    radial_bias,
    radial_out,
    atom_in,
    atom_bias,
    atom_out,
    readout_in,
    readout_out,
):
    dims = scalars.shape[:3]
    slots, width = scalars.shape[3:]
    level = counts.reshape(-1)
    rows = positions.reshape(-1, 1, slots)
    states = [
        scalars.transpose(2, 1, 0, 3, 4)[:, :, :, None],
        vectors.transpose(2, 1, 0, 4, 3, 5),
    ]
    params = (radial_out, atom_in, atom_out, atom_bias, readout_in.T, readout_out[None, :])
    near, tiles, near_counts, blocks = extended(
        states, dims, 0, (level, rows, radial_in, radial_bias)
    )
    params = (blocks,) + params
    layers = radial_in.shape[0]
    turned = dims[::-1]
    for layer in range(layers):
        made = layer_update(layer, dims, radial_in.shape[1], near_counts, tiles, near, params)
        if layer < layers - 1:
            (near,) = extended([made[0].reshape(turned + (4, slots, width))], dims, layer + 1)
    new_scalars, new_vectors, part = made
    scalar_state = new_scalars.reshape(turned + (slots, width)).transpose(2, 1, 0, 3, 4)
    vector_state = new_vectors.reshape(turned + (3, slots, width)).transpose(2, 1, 0, 4, 3, 5)
    energy = summed(part, ("gx", "gy", "gz"), layers)
    return (scalar_state, vector_state, energy)


def solution(mesh):
    block = P("gx", "gy", "gz")
    in_specs = (block,) * 4 + (P(),) * 8
    out_specs = (block, block, P())
    return jax.shard_map(
        on_device, mesh=mesh, in_specs=in_specs, out_specs=out_specs, check_vma=False
    )
```

```python
import functools
import itertools
import math

import jax
import jax.numpy as jnp
from jax import lax
from jax.experimental import pallas as pl
from jax.experimental.pallas import tpu as pltpu
from jax.sharding import PartitionSpec as P

cutoff = 5.0
message_scale = 0.5
group = 8
chunk = 512
table_chunk = 512
shares = 4

MESH = pl.DeviceIdType.MESH


def beside(axis, step):
    count = lax.axis_size(axis)
    return lax.rem(lax.axis_index(axis) + step + count, count)


def prepare(near_ground, radial_in, radial_bias, tiles, counts, radial_block, slots):
    tall, deep, wide = near_ground.shape[:3]
    cells = tall * deep * wide
    rows = near_ground[...].reshape(cells, 128)
    cell = lax.broadcasted_iota(jnp.int32, (cells, 128), 0)
    places = (lax.rem(cell, wide), lax.rem(lax.div(cell, wide), deep), lax.div(cell, wide * deep))
    tiles[...] = jnp.zeros(tiles.shape, tiles.dtype)
    for part in range(3):
        turned = rows
        if part:
            turned = jnp.concatenate([rows[:, part * slots :], rows[:, : part * slots]], axis=1)
        tiles[:, part, :] = turned + (places[part] - 1).astype(jnp.float32) * cutoff
    level = jnp.concatenate([rows[:, 3 * slots :], rows[:, : 3 * slots]], axis=1)
    level = jnp.concatenate([level, jnp.zeros((128 - cells, 128), jnp.float32)], axis=0)
    counts[...] = level.T[:1, :].astype(jnp.int32)

    layers, basis_count, hidden_width = radial_in.shape
    box = (group, hidden_width, 128)
    owner = lax.div(lax.broadcasted_iota(jnp.int32, box, 2), basis_count)
    match = owner == lax.broadcasted_iota(jnp.int32, box, 0)
    column = lax.broadcasted_iota(jnp.int32, (hidden_width, 128), 1) - group * basis_count
    for layer in range(layers):
        small = 0.5 * radial_in[layer].astype(jnp.float32)
        tall_form = jnp.concatenate([small] * (128 // basis_count), axis=0)
        wide_form = jnp.concatenate([tall_form] * (128 // hidden_width), axis=1).T[:hidden_width]
        bias = 0.5 * radial_bias[layer : layer + 1, :]
        bias = jnp.concatenate([bias] * (128 // hidden_width), axis=1)
        bias = jnp.broadcast_to(bias, (128, 128)).T[:hidden_width]
        high = bias.astype(jnp.bfloat16).astype(jnp.float32)
        middle = (bias - high).astype(jnp.bfloat16).astype(jnp.float32)
        low = bias - high - middle
        offset = jnp.where(
            column == 0, high, jnp.where(column == 1, middle, jnp.where(column == 2, low, 0.0))
        )
        spread = jnp.where(match, jnp.broadcast_to(wide_form[None], box), 0.0) + offset[None]
        radial_block[layer] = spread.reshape(radial_block.shape[1:]).astype(jnp.bfloat16)


def halo_kernel(first, dims, *refs):
    wide, deep, tall = dims
    if first:
        scalars, vectors = refs[2:4]
        near = refs[6]
        near_ground = refs[10]
        level, positions, radial_in, radial_bias = refs[11:15]
        results = refs[15:18]
        own_sem, send_sem, recv_sem = refs[18:]
        held = ((scalars, pl.ds(0, 1)), (vectors, pl.ds(1, 3)))
    else:
        block, near, own_sem, send_sem, recv_sem = refs
        held = ((block, pl.ds(0, 4)),)
    barrier = pltpu.get_barrier_semaphore()
    for axis in ("gy", "gx", "gz"):
        for step in (-1, 1):
            pl.semaphore_signal(
                barrier, inc=1, device_id={axis: beside(axis, step)}, device_id_type=MESH
            )
    extents = {"gz": tall, "gy": deep, "gx": wide}
    axes = ("gz", "gy", "gx")
    inner = tuple(pl.ds(1, extents[axis]) for axis in axes)
    own = []
    for place, (state, part) in enumerate(held):
        own.append(
            pltpu.make_async_copy(state, near.at[inner + (part,)], own_sem.at[place])
        )
        own[-1].start()
    if first:
        fetches = []
        sources = refs[:2] + refs[4:6]
        for place, (source, target) in enumerate(zip(sources, refs[11:15])):
            fetches.append(pltpu.make_async_copy(source, target, own_sem.at[2 + place]))
            fetches[-1].start()
        for copy in fetches:
            copy.wait()
        slots = positions.shape[-1]
        for z, y, x in itertools.product(range(tall), range(deep), range(wide)):
            at = (x * deep + y) * tall + z
            row = [positions[at * 3 + k] for k in range(3)]
            row.append(jnp.full((1, 128 - 3 * slots), level[at], jnp.int32).astype(jnp.float32))
            near_ground[z + 1, y + 1, x + 1] = jnp.concatenate(row, axis=1)
    pl.semaphore_wait(barrier, 6)

    copies = []

    def send(ref, start, axis, step, region):
        extent = extents[axis]
        source, target = (extent, 0) if step > 0 else (1, extent + 1)
        return post(ref, start, axis, step, source, target, region)

    def post(ref, start, axis, step, source, target, region):
        begin, end = dict(region), dict(region)
        begin[axis], end[axis] = pl.ds(source, 1), pl.ds(target, 1)
        begin = [begin[name] for name in axes]
        if start is not None:
            begin = [pl.ds(at.start - 1, at.size) for at in begin]
        number = len(copies)
        copy = pltpu.make_async_remote_copy(
            src_ref=(ref if start is None else start).at[tuple(begin)],
            dst_ref=ref.at[tuple(end[name] for name in axes)],
            send_sem=send_sem.at[number],
            recv_sem=recv_sem.at[number],
            device_id={axis: beside(axis, step)},
            device_id_type=MESH,
        )
        copy.start()
        copies.append(copy)
        return copy

    def both(ref, start, axis, region):
        return [send(ref, start, axis, step, region) for step in (-1, 1)]

    def arrive(sent):
        for copy in sent:
            copy.wait_recv()

    odd = lax.rem(lax.axis_index("gz"), 2)
    own_part = {axis: pl.ds(1, extents[axis]) for axis in axes}
    every = {axis: pl.ds(0, extents[axis] + 2) for axis in axes}
    edge = {axis: {-1: pl.ds(extents[axis] + 1, 1), 1: pl.ds(0, 1)} for axis in axes}
    last = []

    mate = 1 - 2 * odd

    def aside(ref, start, step, region):
        flip = odd if step > 0 else 1 - odd
        source, target = tall + flip * (1 - tall), flip * (tall + 1)
        return post(ref, start, "gz", step * mate, source, target, region)

    def begin(axis, step, out, region):
        if not first:
            return [out(near, block, axis, step, region)]
        return [
            out(near.at[:, :, :, part], state, axis, step, region)
            for state, part in ((vectors, pl.ds(1, 3)), (scalars, pl.ds(0, 1)))
        ]

    def sideways(ref, start, axis, step, region):
        return aside(ref, start, step, region)

    def outward(x, region):
        steps = [step for step, place in ((-1, 1), (1, wide)) if place == x]
        return [(step, send(near, None, "gx", step, region)) for step in steps]

    sides = [(x, step) for x in range(1, wide + 1) for step in (-1, 1)]
    along_y, along_x = {}, {}
    if first:
        ground_y = both(near_ground, None, "gy", own_part)
    for x, step in sides:
        along_y[x, step] = begin("gy", step, send, {**own_part, "gx": pl.ds(x, 1)})
    last += begin("gz", -1, sideways, own_part)
    for step in (-1, 1):
        along_x[step] = begin("gx", step, send, own_part)
    if first:
        arrive(ground_y)
        ground_x = both(near_ground, None, "gx", {**own_part, "gy": every["gy"]})
    for step in (-1, 1):
        arrive(along_x[step])
        last.append(aside(near, None, -1, {**own_part, "gx": edge["gx"][step]}))
    for copy in own:
        copy.wait()
    last.append(aside(near, None, 1, {**own_part, "gx": every["gx"]}))
    crossed, turned = {}, {-1: [], 1: []}
    for x, step in sides:
        arrive(along_y[x, step])
        region = {**own_part, "gy": edge["gy"][step], "gx": pl.ds(x, 1)}
        crossed[x, step] = aside(near, None, -1, region)
        turned[step] += [copy for _, copy in outward(x, region)]
    if first:
        arrive(ground_x)
        last_ground = both(near_ground, None, "gz", {**every})
    far = pl.ds(odd * (tall + 1), 1)
    for (x, step), copy in crossed.items():
        arrive([copy])
        region = {"gy": edge["gy"][step], "gx": pl.ds(x, 1), "gz": far}
        last += [copy for _, copy in outward(x, region)]
    for step in (-1, 1):
        arrive(turned[step])
        region = {**own_part, "gy": edge["gy"][step], "gx": every["gx"]}
        last.append(aside(near, None, 1, region))
    if first:
        arrive(last_ground)
        prepare(near_ground, radial_in, radial_bias, *results, slots)
        made = []
        for place, (source, target) in enumerate(zip(results, refs[7:10])):
            made.append(pltpu.make_async_copy(source, target, own_sem.at[6 + place]))
            made[-1].start()
        for copy in made:
            copy.wait()
    arrive(last)
    for copy in copies:
        copy.wait_send()


def extended(states, dims, identity, extra=()):
    wide, deep, tall = dims
    slots, width = states[0].shape[-2:]
    anywhere = pl.BlockSpec(memory_space=pl.ANY)
    outer = (tall + 2, deep + 2, wide + 2)
    cells = math.prod(outer)
    shapes = [jax.ShapeDtypeStruct(outer + (4, slots, width), states[0].dtype)]
    scratch = []
    pieces = 16 + 4 * wide
    if extra:
        layers, basis_count, hidden_width = extra[2].shape
        shapes += [
            jax.ShapeDtypeStruct((cells, 8, 128), jnp.float32),
            jax.ShapeDtypeStruct((1, 128), jnp.int32),
            jax.ShapeDtypeStruct((layers, group * hidden_width, 128), jnp.bfloat16),
        ]
        states = tuple(extra[:2]) + tuple(states) + tuple(extra[2:])
        scratch = [pltpu.VMEM(outer + (1, 128), jnp.float32)]
        scratch.append(pltpu.SMEM(extra[0].shape, extra[0].dtype))
        scratch += [pltpu.VMEM(array.shape, array.dtype) for array in extra[1:]]
        scratch += [pltpu.VMEM(shape.shape, shape.dtype) for shape in shapes[1:]]
        pieces += 6 + 3 + 2 * wide
    return pl.pallas_call(
        functools.partial(halo_kernel, bool(extra), dims),
        out_shape=shapes,
        in_specs=[anywhere] * len(states),
        out_specs=[anywhere] * len(shapes),
        scratch_shapes=scratch
        + [
            pltpu.SemaphoreType.DMA((9,)),
            pltpu.SemaphoreType.DMA((pieces,)),
            pltpu.SemaphoreType.DMA((pieces,)),
        ],
        compiler_params=pltpu.CompilerParams(
            collective_id=identity, has_side_effects=True, vmem_limit_bytes=56 << 20
        ),
        name="halo",
    )(*states)


def total_kernel(axes, part, out, held, local_sem, send_sem, recv_sem):
    sizes = [lax.axis_size(axis) for axis in axes]
    partners = []
    order = sorted(
        itertools.product(*(range(size) for size in sizes)),
        key=lambda steps: -sum(min(step, size - step) for step, size in zip(steps, sizes)),
    )
    for steps in order:
        if any(steps):
            partners.append({axis: beside(axis, step) for axis, step in zip(axes, steps)})
    barrier = pltpu.get_barrier_semaphore()
    for device in partners:
        pl.semaphore_signal(barrier, inc=1, device_id=device, device_id_type=MESH)
    own = pltpu.make_async_copy(part, held.at[pl.ds(0, 1)], local_sem)
    own.start()
    pl.semaphore_wait(barrier, len(partners))
    for place, device in enumerate(partners):
        pltpu.make_async_remote_copy(
            src_ref=part,
            dst_ref=held.at[pl.ds(place + 1, 1)],
            send_sem=send_sem,
            recv_sem=recv_sem,
            device_id=device,
            device_id_type=MESH,
        ).start()
    own.wait()
    rest = held.at[pl.ds(1, len(partners))]
    pltpu.make_async_copy(rest, rest, recv_sem).wait()
    pltpu.make_async_copy(rest, rest, send_sem).wait()
    out[0] = jnp.sum(held[...])


def summed(part, axes, identity):
    count = math.prod(lax.axis_size(axis) for axis in axes)
    return pl.pallas_call(
        functools.partial(total_kernel, axes),
        out_shape=jax.ShapeDtypeStruct((1,), part.dtype),
        in_specs=[pl.BlockSpec(memory_space=pl.ANY)],
        out_specs=pl.BlockSpec(memory_space=pltpu.SMEM),
        scratch_shapes=[
            pltpu.VMEM((count,) + part.shape[1:], part.dtype),
            pltpu.SemaphoreType.DMA,
            pltpu.SemaphoreType.DMA,
            pltpu.SemaphoreType.DMA,
        ],
        compiler_params=pltpu.CompilerParams(
            collective_id=identity, has_side_effects=True, vmem_limit_bytes=56 << 20
        ),
        name="total",
    )(part)


def layer_kernel(dims, basis_count, layer, last, *refs):
    fetched = refs[:10]
    if last:
        scalars_out, vectors_out, part_out = refs[10:13]
    else:
        (block_out,) = refs[10:11]
    counts, tiles, near, radial_block, radial_out, atom_in, atom_out = refs[-21:-14]
    atom_bias_all, readout_in, readout_out = refs[-14:-11]
    fresh, near_place, spots, near_state, edges = refs[-11:-6]
    plain_table, turned_table, marks, agenda, slab_sem, fetch_sem = refs[-6:]
    wide, deep, tall = dims
    slots, width = near.shape[4:]
    hidden_width = radial_out.shape[0]

    whole_near = fetched[2]
    slabs, fetches = [], []
    for place, target in enumerate((counts, tiles)):
        fetches.append(pltpu.make_async_copy(fetched[place], target, fetch_sem.at[place]))
        fetches[-1].start()
    for x in range(wide + 2):
        copy = pltpu.make_async_copy(whole_near.at[:, :, x], near.at[:, :, x], slab_sem.at[x])
        copy.start()
        slabs.append(copy)
    weights = (radial_block, radial_out, atom_in, atom_out, atom_bias_all, readout_in, readout_out)
    for place, (source, target) in enumerate(zip(fetched[3:], weights)):
        if place < 4:
            source = source.at[layer]
        copy = pltpu.make_async_copy(source, target, fetch_sem.at[place + 2])
        copy.start()
        fetches.append(copy)

    inside = [
        (x, y, z)
        for z in range(1, tall + 1)
        for y in range(1, deep + 1)
        for x in range(1, wide + 1)
    ]
    order = list(itertools.product(range(wide + 2), range(deep + 2), range(tall + 2)))

    def index_of(place):
        x, y, z = place
        return (z * (deep + 2) + y) * (wide + 2) + x

    total = 0
    starts = {}
    bounds = [0]
    for copy in fetches[:2]:
        copy.wait()
    for place in order:
        starts[place] = total
        near_place[pl.ds(total, slots), :8] = tiles[index_of(place)].T[:slots, :]
        total = total + counts[0, index_of(place)]
        if place[1:] == (deep + 1, tall + 1):
            bounds.append(total)
    blank = jnp.zeros((table_chunk, width), jnp.float32)
    window = spots.shape[3]
    near_place[pl.ds(total, window), :] = jnp.zeros((window, width), jnp.float32)
    chunks = lax.div(total + table_chunk - 1, table_chunk)
    for number, place in enumerate(inside):
        x = place[0]
        base = lax.div(bounds[x - 1], 16) * 16
        steps = lax.div(bounds[x + 2] - base + chunk - 1, chunk)
        marks[number, 0] = jnp.clip(chunks * table_chunk - steps * chunk, 0, base)
        marks[number, 1] = steps
        marks[number, 2] = starts[place]
        marks[number, 3] = counts[0, index_of(place)]

    quarter = math.pi / cutoff
    sharpness = 0.5 * ((basis_count - 1) / cutoff) ** 2
    tile = 16
    fresh[...] = jnp.zeros(fresh.shape, fresh.dtype)

    longest = functools.reduce(jnp.maximum, [marks[number, 1] for number in range(len(inside))])

    @pl.loop(0, longest)
    def _(step):
        columns = pl.ds(pl.multiple_of(step * chunk, chunk), chunk)
        for number in range(len(inside)):
            begin = marks[number, 0] + step * chunk
            start = marks[number, 2]
            line = near_place[pl.ds(begin, chunk), :].T[:8, :]
            mine = near_place[pl.ds(start, slots), :]
            col = begin + lax.broadcasted_iota(jnp.int32, (slots, chunk), 1)
            row = start + lax.broadcasted_iota(jnp.int32, (slots, chunk), 0)
            unused = jnp.logical_or(col == row, col >= total)
            offset = [line[k : k + 1, :] - mine[:, k : k + 1] for k in range(3)]
            square = offset[0] * offset[0] + offset[1] * offset[1] + offset[2] * offset[2]
            square = square + jnp.where(unused, 1.0, 0.0)
            inverse = lax.rsqrt(square)
            distance = square * inverse
            angle = quarter * distance - 0.5 * math.pi
            turn = angle * angle
            series = 0.0
            for power in (13, 11, 9, 7, 5, 3):
                series = turn * (series + (-1.0) ** (power // 2) / math.factorial(power))
            smooth = 0.5 - 0.5 * (angle + angle * series)
            spots[number, 0, :, columns] = distance
            spots[number, 1, :, columns] = jnp.where(
                jnp.logical_and(distance < cutoff, jnp.logical_not(unused)), smooth, 0.0
            )
            for k in range(3):
                spots[number, k + 2, :, columns] = offset[k] * inverse

    for place in order:
        x, y, z = place
        if (y, z) == (0, 0):
            slabs[x].wait()
        for part in range(4):
            near_state[part, pl.ds(starts[place], slots), :] = near[z, y, x, part].astype(
                jnp.float32
            )
    for part in range(4):
        near_state[part, pl.ds(total, table_chunk), :] = blank
    for copy in fetches[2:]:
        copy.wait()

    @pl.loop(0, chunks)
    def _(step):
        rows = pl.ds(pl.multiple_of(step * table_chunk, table_chunk), table_chunk)
        half = jnp.dot(
            near_state[0, rows, :].astype(jnp.bfloat16),
            (0.5 * atom_in[...].astype(jnp.float32)).astype(jnp.bfloat16),
            preferred_element_type=jnp.float32,
        ) + 0.5 * atom_bias_all[layer : layer + 1, :]
        hidden = (half + half * jnp.tanh(half)).astype(jnp.bfloat16)
        gates = jnp.dot(hidden, atom_out[...], preferred_element_type=jnp.float32).astype(
            jnp.bfloat16
        )
        plain_table[rows, :width] = gates[:, :width]
        gate_b = gates[:, width : 2 * width].astype(jnp.float32)
        gate_c = gates[:, 2 * width : 3 * width]
        gate_g = gates[:, 3 * width :].astype(jnp.float32)
        for part in range(3):
            vector = near_state[part + 1, rows, :]
            plain_table[rows, (part + 1) * width : (part + 2) * width] = (gate_b * vector).astype(
                jnp.bfloat16
            )
            turned_table[part, rows, :width] = gate_c
            turned_table[part, rows, width:] = (gate_g * vector).astype(jnp.bfloat16)

    tasks = 0
    for number in range(len(inside)):
        steps = marks[number, 1]
        turns = lax.div(marks[number, 3] + group - 1, group)

        @pl.loop(0, turns * steps)
        def _(task, number=number, steps=steps, tasks=tasks):
            turn = lax.div(task, steps)
            agenda[tasks + task, 0] = number
            agenda[tasks + task, 1] = turn * group
            agenda[tasks + task, 2] = task - turn * steps

        tasks = tasks + turns * steps

    share = group // shares

    def spread_basis(task):
        number = agenda[task, 0]
        these = pl.ds(pl.multiple_of(agenda[task, 1], group), group)
        columns = pl.ds(pl.multiple_of(agenda[task, 2] * chunk, chunk), chunk)
        centers = lax.broadcasted_iota(jnp.int32, (1, basis_count, chunk), 1).astype(
            jnp.float32
        ) * (cutoff / (basis_count - 1))
        gap = spots[number, 0, these, columns][:, None, :] - centers
        basis = jnp.exp(-sharpness * gap * gap).reshape(group * basis_count, chunk)
        return jnp.concatenate(
            [basis, jnp.ones((128 - group * basis_count, chunk), jnp.float32)], axis=0
        ).astype(jnp.bfloat16)

    def form_edges(task, basis, part, edges):
        number = agenda[task, 0]
        these = pl.ds(pl.multiple_of(agenda[task, 1], group), group)
        columns = pl.ds(pl.multiple_of(agenda[task, 2] * chunk, chunk), chunk)
        mine = slice(part * share, (part + 1) * share)
        rows = slice(part * share * hidden_width, (part + 1) * share * hidden_width)
        half = jnp.dot(
            radial_block[rows, :], basis, preferred_element_type=jnp.float32
        ).reshape(share, hidden_width, chunk)
        weight = spots[number, 1, these, columns][mine, None, :]
        active = (half + half * jnp.tanh(half)) * weight
        active = active.astype(jnp.bfloat16).reshape(share, hidden_width // tile, tile, chunk)
        edges[0, rows, :] = active.reshape(share * hidden_width, chunk)
        for k in range(3):
            unit = jnp.broadcast_to(
                spots[number, k + 2, these, columns][mine, None, :], (share, tile, chunk)
            ).astype(jnp.bfloat16)
            edges[k + 1, rows, :] = (active * unit[:, None]).reshape(share * hidden_width, chunk)

    def contract(task, edges):
        number = agenda[task, 0]
        these = pl.ds(pl.multiple_of(agenda[task, 1], group), group)
        rows = pl.ds(pl.multiple_of(marks[number, 0] + agenda[task, 2] * chunk, 16), chunk)

        def contracted(left, right, filters):
            product = jnp.dot(left, right, preferred_element_type=jnp.float32)
            product = product.reshape(group, hidden_width, 2 * width)
            return (
                jnp.sum(product[:, :, :width] * filters[0], axis=1),
                jnp.sum(product[:, :, width:] * filters[1], axis=1),
            )

        bank = [
            radial_out[:, part * width : (part + 1) * width].astype(jnp.float32)[None]
            for part in range(4)
        ]
        scalar, vector0 = contracted(edges[0], plain_table[rows, : 2 * width], (bank[0], bank[1]))
        vector1, vector2 = contracted(edges[0], plain_table[rows, 2 * width :], (bank[1], bank[1]))
        vectors = [vector0, vector1, vector2]
        for k in range(3):
            along, project = contracted(edges[k + 1], turned_table[k, rows, :], (bank[2], bank[3]))
            vectors[k] = vectors[k] + along
            scalar = scalar + project
        for part, change in enumerate([scalar] + vectors):
            fresh[number, part, these, :] += change

    @pl.loop(0, tasks)
    def _(task):
        basis = spread_basis(task)
        for part in range(shares):
            form_edges(task, basis, part, edges)
        contract(task, edges)

    energy = jnp.zeros((1, 1), jnp.float32)
    for number, place in enumerate(inside):
        alive = (
            lax.broadcasted_iota(jnp.int32, (slots, width), 0) < counts[0, index_of(place)]
        )
        rounded = [
            jnp.where(
                alive,
                near_state[part, pl.ds(starts[place], slots), :]
                + message_scale * fresh[number, part],
                0.0,
            ).astype(jnp.bfloat16)
            for part in range(4)
        ]
        if last:
            scalars_out[number] = rounded[0]
            for part in range(3):
                vectors_out[number, part] = rounded[part + 1]
            read = lax.dot_general(
                rounded[0],
                readout_in[...],
                (((1,), (1,)), ((), ())),
                preferred_element_type=jnp.float32,
            )
            read = read / (1.0 + jnp.exp(-read)) * readout_out[...]
            read = jnp.where(alive[:, : read.shape[1]], read, 0.0)
            energy = energy + jnp.sum(read, axis=(0, 1), keepdims=True)
        else:
            for part in range(4):
                block_out[number, part] = rounded[part]
    if last:
        spot = lax.broadcasted_iota(jnp.int32, part_out.shape, 1)
        part_out[...] = jnp.where(spot == 0, jnp.broadcast_to(energy, part_out.shape), 0.0)


def layer_update(layer, dims, basis_count, counts, tiles, near, params):
    wide, deep, tall = dims
    radial_out = params[1]
    around = math.prod(near.shape[:3])
    slots, width = near.shape[4:]
    hidden_width = radial_out.shape[1]
    last = layer == radial_out.shape[0] - 1
    cells = wide * deep * tall
    span = -(-around * slots // table_chunk) * table_chunk + chunk - table_chunk
    window = -(-(3 * (around // (wide + 2)) * slots + 16) // chunk) * chunk
    store = around * slots + window + slots
    vmem = pl.BlockSpec(memory_space=pltpu.VMEM)
    anywhere = pl.BlockSpec(memory_space=pl.ANY)
    if last:
        shapes = (
            jax.ShapeDtypeStruct((cells, slots, width), jnp.bfloat16),
            jax.ShapeDtypeStruct((cells, 3, slots, width), jnp.bfloat16),
            jax.ShapeDtypeStruct((1, 128), jnp.float32),
        )
    else:
        shapes = (jax.ShapeDtypeStruct((cells, 4, slots, width), jnp.bfloat16),)
    fetched = (counts, tiles, near) + params
    return pl.pallas_call(
        functools.partial(layer_kernel, dims, basis_count, layer, last),
        out_shape=shapes,
        in_specs=[anywhere] * len(fetched),
        out_specs=tuple(vmem for _ in shapes),
        scratch_shapes=[pltpu.SMEM(counts.shape, counts.dtype)]
        + [pltpu.VMEM(array.shape, array.dtype) for array in fetched[1:3]]
        + [pltpu.VMEM(array.shape[1:], array.dtype) for array in params[:4]]
        + [pltpu.VMEM(array.shape, array.dtype) for array in params[4:]]
        + [
            pltpu.VMEM((cells, 4, slots, width), jnp.float32),
            pltpu.VMEM((store, width), jnp.float32),
            pltpu.VMEM((cells, 5, slots, window), jnp.float32),
            pltpu.VMEM((4, store, width), jnp.float32),
            pltpu.VMEM((4, group * hidden_width, chunk), jnp.bfloat16),
            pltpu.VMEM((span, 4 * width), jnp.bfloat16),
            pltpu.VMEM((3, span, 2 * width), jnp.bfloat16),
            pltpu.SMEM((cells, 4), jnp.int32),
            pltpu.SMEM((cells * (slots // group) * (window // chunk), 3), jnp.int32),
            pltpu.SemaphoreType.DMA((wide + 2,)),
            pltpu.SemaphoreType.DMA((9,)),
        ],
        compiler_params=pltpu.CompilerParams(vmem_limit_bytes=56 << 20),
        name="message_layer",
    )(*fetched)


def on_device(
    positions,
    counts,
    scalars,
    vectors,
    radial_in,
    radial_bias,
    radial_out,
    atom_in,
    atom_bias,
    atom_out,
    readout_in,
    readout_out,
):
    dims = scalars.shape[:3]
    slots, width = scalars.shape[3:]
    level = counts.reshape(-1)
    rows = positions.reshape(-1, 1, slots)
    states = [
        scalars.transpose(2, 1, 0, 3, 4)[:, :, :, None],
        vectors.transpose(2, 1, 0, 4, 3, 5),
    ]
    params = (radial_out, atom_in, atom_out, atom_bias, readout_in.T, readout_out[None, :])
    near, tiles, near_counts, blocks = extended(
        states, dims, 0, (level, rows, radial_in, radial_bias)
    )
    params = (blocks,) + params
    layers = radial_in.shape[0]
    turned = dims[::-1]
    for layer in range(layers):
        made = layer_update(layer, dims, radial_in.shape[1], near_counts, tiles, near, params)
        if layer < layers - 1:
            (near,) = extended([made[0].reshape(turned + (4, slots, width))], dims, layer + 1)
    new_scalars, new_vectors, part = made
    scalar_state = new_scalars.reshape(turned + (slots, width)).transpose(2, 1, 0, 3, 4)
    vector_state = new_vectors.reshape(turned + (3, slots, width)).transpose(2, 1, 0, 4, 3, 5)
    energy = summed(part, ("gx", "gy", "gz"), layers)
    return (scalar_state, vector_state, energy)


def solution(mesh):
    block = P("gx", "gy", "gz")
    in_specs = (block,) * 4 + (P(),) * 8
    out_specs = (block, block, P())
    return jax.shard_map(
        on_device, mesh=mesh, in_specs=in_specs, out_specs=out_specs, check_vma=False
    )
```

```python
import functools
import itertools
import math

import jax
import jax.numpy as jnp
from jax import lax
from jax.experimental import pallas as pl
from jax.experimental.pallas import tpu as pltpu
from jax.sharding import PartitionSpec as P

cutoff = 5.0
message_scale = 0.5
group = 8
chunk = 512
table_chunk = 512
shares = 4

MESH = pl.DeviceIdType.MESH


def beside(axis, step):
    count = lax.axis_size(axis)
    return lax.rem(lax.axis_index(axis) + step + count, count)


def prepare(near_ground, radial_in, radial_bias, tiles, counts, radial_block, slots):
    tall, deep, wide = near_ground.shape[:3]
    cells = tall * deep * wide
    rows = near_ground[...].reshape(cells, 128)
    cell = lax.broadcasted_iota(jnp.int32, (cells, 128), 0)
    places = (lax.rem(cell, wide), lax.rem(lax.div(cell, wide), deep), lax.div(cell, wide * deep))
    tiles[...] = jnp.zeros(tiles.shape, tiles.dtype)
    for part in range(3):
        turned = rows
        if part:
            turned = jnp.concatenate([rows[:, part * slots :], rows[:, : part * slots]], axis=1)
        tiles[:, part, :] = turned + (places[part] - 1).astype(jnp.float32) * cutoff
    level = jnp.concatenate([rows[:, 3 * slots :], rows[:, : 3 * slots]], axis=1)
    level = jnp.concatenate([level, jnp.zeros((128 - cells, 128), jnp.float32)], axis=0)
    counts[...] = level.T[:1, :].astype(jnp.int32)

    layers, basis_count, hidden_width = radial_in.shape
    box = (group, hidden_width, 128)
    owner = lax.div(lax.broadcasted_iota(jnp.int32, box, 2), basis_count)
    match = owner == lax.broadcasted_iota(jnp.int32, box, 0)
    column = lax.broadcasted_iota(jnp.int32, (hidden_width, 128), 1) - group * basis_count
    for layer in range(layers):
        small = 0.5 * radial_in[layer].astype(jnp.float32)
        tall_form = jnp.concatenate([small] * (128 // basis_count), axis=0)
        wide_form = jnp.concatenate([tall_form] * (128 // hidden_width), axis=1).T[:hidden_width]
        bias = 0.5 * radial_bias[layer : layer + 1, :]
        bias = jnp.concatenate([bias] * (128 // hidden_width), axis=1)
        bias = jnp.broadcast_to(bias, (128, 128)).T[:hidden_width]
        high = bias.astype(jnp.bfloat16).astype(jnp.float32)
        middle = (bias - high).astype(jnp.bfloat16).astype(jnp.float32)
        low = bias - high - middle
        offset = jnp.where(
            column == 0, high, jnp.where(column == 1, middle, jnp.where(column == 2, low, 0.0))
        )
        spread = jnp.where(match, jnp.broadcast_to(wide_form[None], box), 0.0) + offset[None]
        radial_block[layer] = spread.reshape(radial_block.shape[1:]).astype(jnp.bfloat16)


def halo_kernel(first, dims, *refs):
    wide, deep, tall = dims
    if first:
        scalars, vectors = refs[2:4]
        near = refs[6]
        near_ground = refs[10]
        level, positions, radial_in, radial_bias = refs[11:15]
        results = refs[15:18]
        own_sem, send_sem, recv_sem = refs[18:]
        held = ((scalars, pl.ds(0, 1)), (vectors, pl.ds(1, 3)))
    else:
        block, near, own_sem, send_sem, recv_sem = refs
        held = ((block, pl.ds(0, 4)),)
    barrier = pltpu.get_barrier_semaphore()
    for axis in ("gy", "gx", "gz"):
        for step in (-1, 1):
            pl.semaphore_signal(
                barrier, inc=1, device_id={axis: beside(axis, step)}, device_id_type=MESH
            )
    extents = {"gz": tall, "gy": deep, "gx": wide}
    axes = ("gz", "gy", "gx")
    inner = tuple(pl.ds(1, extents[axis]) for axis in axes)
    own = []
    for place, (state, part) in enumerate(held):
        own.append(
            pltpu.make_async_copy(state, near.at[inner + (part,)], own_sem.at[place])
        )
        own[-1].start()
    if first:
        fetches = []
        sources = refs[:2] + refs[4:6]
        for place, (source, target) in enumerate(zip(sources, refs[11:15])):
            fetches.append(pltpu.make_async_copy(source, target, own_sem.at[2 + place]))
            fetches[-1].start()
        for copy in fetches:
            copy.wait()
        slots = positions.shape[-1]
        for z, y, x in itertools.product(range(tall), range(deep), range(wide)):
            at = (x * deep + y) * tall + z
            row = [positions[at * 3 + k] for k in range(3)]
            row.append(jnp.full((1, 128 - 3 * slots), level[at], jnp.int32).astype(jnp.float32))
            near_ground[z + 1, y + 1, x + 1] = jnp.concatenate(row, axis=1)
    pl.semaphore_wait(barrier, 6)

    copies = []

    def send(ref, start, axis, step, region):
        extent = extents[axis]
        source, target = (extent, 0) if step > 0 else (1, extent + 1)
        return post(ref, start, axis, step, source, target, region)

    def post(ref, start, axis, step, source, target, region):
        begin, end = dict(region), dict(region)
        begin[axis], end[axis] = pl.ds(source, 1), pl.ds(target, 1)
        begin = [begin[name] for name in axes]
        if start is not None:
            begin = [pl.ds(at.start - 1, at.size) for at in begin]
        number = len(copies)
        copy = pltpu.make_async_remote_copy(
            src_ref=(ref if start is None else start).at[tuple(begin)],
            dst_ref=ref.at[tuple(end[name] for name in axes)],
            send_sem=send_sem.at[number],
            recv_sem=recv_sem.at[number],
            device_id={axis: beside(axis, step)},
            device_id_type=MESH,
        )
        copy.start()
        copies.append(copy)
        return copy

    def both(ref, start, axis, region):
        return [send(ref, start, axis, step, region) for step in (-1, 1)]

    def arrive(sent):
        for copy in sent:
            copy.wait_recv()

    odd = lax.rem(lax.axis_index("gz"), 2)
    own_part = {axis: pl.ds(1, extents[axis]) for axis in axes}
    every = {axis: pl.ds(0, extents[axis] + 2) for axis in axes}
    edge = {axis: {-1: pl.ds(extents[axis] + 1, 1), 1: pl.ds(0, 1)} for axis in axes}
    last = []

    mate = 1 - 2 * odd

    def aside(ref, start, step, region):
        flip = odd if step > 0 else 1 - odd
        source, target = tall + flip * (1 - tall), flip * (tall + 1)
        return post(ref, start, "gz", step * mate, source, target, region)

    def begin(axis, step, out, region):
        if not first:
            return [out(near, block, axis, step, region)]
        return [
            out(near.at[:, :, :, part], state, axis, step, region)
            for state, part in ((vectors, pl.ds(1, 3)), (scalars, pl.ds(0, 1)))
        ]

    def sideways(ref, start, axis, step, region):
        return aside(ref, start, step, region)

    def outward(x, region):
        steps = [step for step, place in ((-1, 1), (1, wide)) if place == x]
        return [(step, send(near, None, "gx", step, region)) for step in steps]

    sides = [(x, step) for x in range(1, wide + 1) for step in (-1, 1)]
    along_y, along_x = {}, {}
    if first:
        ground_y = both(near_ground, None, "gy", own_part)
    for x, step in sides:
        along_y[x, step] = begin("gy", step, send, {**own_part, "gx": pl.ds(x, 1)})
    last += begin("gz", -1, sideways, own_part)
    for step in (-1, 1):
        along_x[step] = begin("gx", step, send, own_part)
    if first:
        arrive(ground_y)
        ground_x = both(near_ground, None, "gx", {**own_part, "gy": every["gy"]})
    for step in (-1, 1):
        arrive(along_x[step])
        last.append(aside(near, None, -1, {**own_part, "gx": edge["gx"][step]}))
    for copy in own:
        copy.wait()
    last.append(aside(near, None, 1, {**own_part, "gx": every["gx"]}))
    crossed, turned = {}, {-1: [], 1: []}
    for x, step in sides:
        arrive(along_y[x, step])
        region = {**own_part, "gy": edge["gy"][step], "gx": pl.ds(x, 1)}
        crossed[x, step] = aside(near, None, -1, region)
        turned[step] += [copy for _, copy in outward(x, region)]
    if first:
        arrive(ground_x)
        last_ground = both(near_ground, None, "gz", {**every})
    far = pl.ds(odd * (tall + 1), 1)
    for (x, step), copy in crossed.items():
        arrive([copy])
        region = {"gy": edge["gy"][step], "gx": pl.ds(x, 1), "gz": far}
        last += [copy for _, copy in outward(x, region)]
    for step in (-1, 1):
        arrive(turned[step])
        region = {**own_part, "gy": edge["gy"][step], "gx": every["gx"]}
        last.append(aside(near, None, 1, region))
    if first:
        arrive(last_ground)
        prepare(near_ground, radial_in, radial_bias, *results, slots)
        made = []
        for place, (source, target) in enumerate(zip(results, refs[7:10])):
            made.append(pltpu.make_async_copy(source, target, own_sem.at[6 + place]))
            made[-1].start()
        for copy in made:
            copy.wait()
    arrive(last)
    for copy in copies:
        copy.wait_send()


def extended(states, dims, identity, extra=()):
    wide, deep, tall = dims
    slots, width = states[0].shape[-2:]
    anywhere = pl.BlockSpec(memory_space=pl.ANY)
    outer = (tall + 2, deep + 2, wide + 2)
    cells = math.prod(outer)
    shapes = [jax.ShapeDtypeStruct(outer + (4, slots, width), states[0].dtype)]
    scratch = []
    pieces = 16 + 4 * wide
    if extra:
        layers, basis_count, hidden_width = extra[2].shape
        shapes += [
            jax.ShapeDtypeStruct((cells, 8, 128), jnp.float32),
            jax.ShapeDtypeStruct((1, 128), jnp.int32),
            jax.ShapeDtypeStruct((layers, group * hidden_width, 128), jnp.bfloat16),
        ]
        states = tuple(extra[:2]) + tuple(states) + tuple(extra[2:])
        scratch = [pltpu.VMEM(outer + (1, 128), jnp.float32)]
        scratch.append(pltpu.SMEM(extra[0].shape, extra[0].dtype))
        scratch += [pltpu.VMEM(array.shape, array.dtype) for array in extra[1:]]
        scratch += [pltpu.VMEM(shape.shape, shape.dtype) for shape in shapes[1:]]
        pieces += 6 + 3 + 2 * wide
    return pl.pallas_call(
        functools.partial(halo_kernel, bool(extra), dims),
        out_shape=shapes,
        in_specs=[anywhere] * len(states),
        out_specs=[anywhere] * len(shapes),
        scratch_shapes=scratch
        + [
            pltpu.SemaphoreType.DMA((9,)),
            pltpu.SemaphoreType.DMA((pieces,)),
            pltpu.SemaphoreType.DMA((pieces,)),
        ],
        compiler_params=pltpu.CompilerParams(
            collective_id=identity, has_side_effects=True, vmem_limit_bytes=56 << 20
        ),
        name="halo",
    )(*states)


def total_kernel(axes, part, out, held, local_sem, send_sem, recv_sem):
    sizes = [lax.axis_size(axis) for axis in axes]
    partners = []
    order = sorted(
        itertools.product(*(range(size) for size in sizes)),
        key=lambda steps: -sum(min(step, size - step) for step, size in zip(steps, sizes)),
    )
    for steps in order:
        if any(steps):
            partners.append({axis: beside(axis, step) for axis, step in zip(axes, steps)})
    barrier = pltpu.get_barrier_semaphore()
    for device in partners:
        pl.semaphore_signal(barrier, inc=1, device_id=device, device_id_type=MESH)
    own = pltpu.make_async_copy(part, held.at[pl.ds(0, 1)], local_sem)
    own.start()
    pl.semaphore_wait(barrier, len(partners))
    for place, device in enumerate(partners):
        pltpu.make_async_remote_copy(
            src_ref=part,
            dst_ref=held.at[pl.ds(place + 1, 1)],
            send_sem=send_sem,
            recv_sem=recv_sem,
            device_id=device,
            device_id_type=MESH,
        ).start()
    own.wait()
    rest = held.at[pl.ds(1, len(partners))]
    pltpu.make_async_copy(rest, rest, recv_sem).wait()
    pltpu.make_async_copy(rest, rest, send_sem).wait()
    out[0] = jnp.sum(held[...])


def summed(part, axes, identity):
    count = math.prod(lax.axis_size(axis) for axis in axes)
    return pl.pallas_call(
        functools.partial(total_kernel, axes),
        out_shape=jax.ShapeDtypeStruct((1,), part.dtype),
        in_specs=[pl.BlockSpec(memory_space=pl.ANY)],
        out_specs=pl.BlockSpec(memory_space=pltpu.SMEM),
        scratch_shapes=[
            pltpu.VMEM((count,) + part.shape[1:], part.dtype),
            pltpu.SemaphoreType.DMA,
            pltpu.SemaphoreType.DMA,
            pltpu.SemaphoreType.DMA,
        ],
        compiler_params=pltpu.CompilerParams(
            collective_id=identity, has_side_effects=True, vmem_limit_bytes=56 << 20
        ),
        name="total",
    )(part)


def layer_kernel(dims, basis_count, layer, last, *refs):
    fetched = refs[:10]
    if last:
        scalars_out, vectors_out, part_out = refs[10:13]
    else:
        (block_out,) = refs[10:11]
    counts, tiles, near, radial_block, radial_out, atom_in, atom_out = refs[-21:-14]
    atom_bias_all, readout_in, readout_out = refs[-14:-11]
    fresh, near_place, spots, near_state, edges = refs[-11:-6]
    plain_table, turned_table, marks, agenda, slab_sem, fetch_sem = refs[-6:]
    wide, deep, tall = dims
    slots, width = near.shape[4:]
    hidden_width = radial_out.shape[0]

    whole_near = fetched[2]
    slabs, fetches = [], []
    for place, target in enumerate((counts, tiles)):
        fetches.append(pltpu.make_async_copy(fetched[place], target, fetch_sem.at[place]))
        fetches[-1].start()
    for x in range(wide + 2):
        copy = pltpu.make_async_copy(whole_near.at[:, :, x], near.at[:, :, x], slab_sem.at[x])
        copy.start()
        slabs.append(copy)
    weights = (radial_block, radial_out, atom_in, atom_out, atom_bias_all, readout_in, readout_out)
    for place, (source, target) in enumerate(zip(fetched[3:], weights)):
        if place < 4:
            source = source.at[layer]
        copy = pltpu.make_async_copy(source, target, fetch_sem.at[place + 2])
        copy.start()
        fetches.append(copy)

    inside = [
        (x, y, z)
        for z in range(1, tall + 1)
        for y in range(1, deep + 1)
        for x in range(1, wide + 1)
    ]
    order = list(itertools.product(range(wide + 2), range(deep + 2), range(tall + 2)))

    def index_of(place):
        x, y, z = place
        return (z * (deep + 2) + y) * (wide + 2) + x

    total = 0
    starts = {}
    bounds = [0]
    for copy in fetches[:2]:
        copy.wait()
    for place in order:
        starts[place] = total
        near_place[pl.ds(total, slots), :8] = tiles[index_of(place)].T[:slots, :]
        total = total + counts[0, index_of(place)]
        if place[1:] == (deep + 1, tall + 1):
            bounds.append(total)
    blank = jnp.zeros((table_chunk, width), jnp.float32)
    window = spots.shape[3]
    near_place[pl.ds(total, window), :] = jnp.zeros((window, width), jnp.float32)
    chunks = lax.div(total + table_chunk - 1, table_chunk)
    for number, place in enumerate(inside):
        x = place[0]
        base = lax.div(bounds[x - 1], 16) * 16
        steps = lax.div(bounds[x + 2] - base + chunk - 1, chunk)
        marks[number, 0] = jnp.clip(chunks * table_chunk - steps * chunk, 0, base)
        marks[number, 1] = steps
        marks[number, 2] = starts[place]
        marks[number, 3] = counts[0, index_of(place)]

    quarter = math.pi / cutoff
    sharpness = 0.5 * ((basis_count - 1) / cutoff) ** 2
    tile = 16
    fresh[...] = jnp.zeros(fresh.shape, fresh.dtype)

    longest = functools.reduce(jnp.maximum, [marks[number, 1] for number in range(len(inside))])

    @pl.loop(0, longest)
    def _(step):
        columns = pl.ds(pl.multiple_of(step * chunk, chunk), chunk)
        for number in range(len(inside)):
            begin = marks[number, 0] + step * chunk
            start = marks[number, 2]
            line = near_place[pl.ds(begin, chunk), :].T[:8, :]
            mine = near_place[pl.ds(start, slots), :]
            col = begin + lax.broadcasted_iota(jnp.int32, (slots, chunk), 1)
            row = start + lax.broadcasted_iota(jnp.int32, (slots, chunk), 0)
            unused = jnp.logical_or(col == row, col >= total)
            offset = [line[k : k + 1, :] - mine[:, k : k + 1] for k in range(3)]
            square = offset[0] * offset[0] + offset[1] * offset[1] + offset[2] * offset[2]
            square = square + jnp.where(unused, 1.0, 0.0)
            inverse = lax.rsqrt(square)
            distance = square * inverse
            angle = quarter * distance - 0.5 * math.pi
            turn = angle * angle
            series = 0.0
            for power in (13, 11, 9, 7, 5, 3):
                series = turn * (series + (-1.0) ** (power // 2) / math.factorial(power))
            smooth = 0.5 - 0.5 * (angle + angle * series)
            spots[number, 0, :, columns] = distance
            spots[number, 1, :, columns] = jnp.where(
                jnp.logical_and(distance < cutoff, jnp.logical_not(unused)), smooth, 0.0
            )
            for k in range(3):
                spots[number, k + 2, :, columns] = offset[k] * inverse

    for place in order:
        x, y, z = place
        if (y, z) == (0, 0):
            slabs[x].wait()
        for part in range(4):
            near_state[part, pl.ds(starts[place], slots), :] = near[z, y, x, part].astype(
                jnp.float32
            )
    for part in range(4):
        near_state[part, pl.ds(total, table_chunk), :] = blank
    for copy in fetches[2:]:
        copy.wait()

    @pl.loop(0, chunks)
    def _(step):
        rows = pl.ds(pl.multiple_of(step * table_chunk, table_chunk), table_chunk)
        half = jnp.dot(
            near_state[0, rows, :].astype(jnp.bfloat16),
            (0.5 * atom_in[...].astype(jnp.float32)).astype(jnp.bfloat16),
            preferred_element_type=jnp.float32,
        ) + 0.5 * atom_bias_all[layer : layer + 1, :]
        hidden = (half + half * jnp.tanh(half)).astype(jnp.bfloat16)
        gates = jnp.dot(hidden, atom_out[...], preferred_element_type=jnp.float32).astype(
            jnp.bfloat16
        )
        plain_table[rows, :width] = gates[:, :width]
        gate_b = gates[:, width : 2 * width].astype(jnp.float32)
        gate_c = gates[:, 2 * width : 3 * width]
        gate_g = gates[:, 3 * width :].astype(jnp.float32)
        for part in range(3):
            vector = near_state[part + 1, rows, :]
            plain_table[rows, (part + 1) * width : (part + 2) * width] = (gate_b * vector).astype(
                jnp.bfloat16
            )
            turned_table[part, rows, :width] = gate_c
            turned_table[part, rows, width:] = (gate_g * vector).astype(jnp.bfloat16)

    tasks = 0
    for number in range(len(inside)):
        steps = marks[number, 1]
        turns = lax.div(marks[number, 3] + group - 1, group)

        @pl.loop(0, turns * steps)
        def _(task, number=number, steps=steps, tasks=tasks):
            turn = lax.div(task, steps)
            agenda[tasks + task, 0] = number
            agenda[tasks + task, 1] = turn * group
            agenda[tasks + task, 2] = task - turn * steps

        tasks = tasks + turns * steps

    share = group // shares

    def spread_basis(task):
        number = agenda[task, 0]
        these = pl.ds(pl.multiple_of(agenda[task, 1], group), group)
        columns = pl.ds(pl.multiple_of(agenda[task, 2] * chunk, chunk), chunk)
        centers = lax.broadcasted_iota(jnp.int32, (1, basis_count, chunk), 1).astype(
            jnp.float32
        ) * (cutoff / (basis_count - 1))
        gap = spots[number, 0, these, columns][:, None, :] - centers
        basis = jnp.exp(-sharpness * gap * gap).reshape(group * basis_count, chunk)
        return jnp.concatenate(
            [basis, jnp.ones((128 - group * basis_count, chunk), jnp.float32)], axis=0
        ).astype(jnp.bfloat16)

    def form_edges(task, basis, part, edges):
        number = agenda[task, 0]
        these = pl.ds(pl.multiple_of(agenda[task, 1], group), group)
        columns = pl.ds(pl.multiple_of(agenda[task, 2] * chunk, chunk), chunk)
        mine = slice(part * share, (part + 1) * share)
        rows = slice(part * share * hidden_width, (part + 1) * share * hidden_width)
        half = jnp.dot(
            radial_block[rows, :], basis, preferred_element_type=jnp.float32
        ).reshape(share, hidden_width, chunk)
        weight = spots[number, 1, these, columns][mine, None, :]
        active = (half + half * jnp.tanh(half)).astype(jnp.bfloat16)
        active = active.reshape(share, hidden_width // tile, tile, chunk)
        weight = jnp.broadcast_to(weight, (share, tile, chunk)).astype(jnp.bfloat16)
        active = active * weight[:, None]
        edges[0, rows, :] = active.reshape(share * hidden_width, chunk)
        for k in range(3):
            unit = jnp.broadcast_to(
                spots[number, k + 2, these, columns][mine, None, :], (share, tile, chunk)
            ).astype(jnp.bfloat16)
            edges[k + 1, rows, :] = (active * unit[:, None]).reshape(share * hidden_width, chunk)

    def contract(task, edges):
        number = agenda[task, 0]
        these = pl.ds(pl.multiple_of(agenda[task, 1], group), group)
        rows = pl.ds(pl.multiple_of(marks[number, 0] + agenda[task, 2] * chunk, 16), chunk)

        def contracted(left, right, filters):
            product = jnp.dot(left, right, preferred_element_type=jnp.float32)
            product = product.reshape(group, hidden_width, 2 * width)
            return (
                jnp.sum(product[:, :, :width] * filters[0], axis=1),
                jnp.sum(product[:, :, width:] * filters[1], axis=1),
            )

        bank = [
            radial_out[:, part * width : (part + 1) * width].astype(jnp.float32)[None]
            for part in range(4)
        ]
        scalar, vector0 = contracted(edges[0], plain_table[rows, : 2 * width], (bank[0], bank[1]))
        vector1, vector2 = contracted(edges[0], plain_table[rows, 2 * width :], (bank[1], bank[1]))
        vectors = [vector0, vector1, vector2]
        for k in range(3):
            along, project = contracted(edges[k + 1], turned_table[k, rows, :], (bank[2], bank[3]))
            vectors[k] = vectors[k] + along
            scalar = scalar + project
        for part, change in enumerate([scalar] + vectors):
            fresh[number, part, these, :] += change

    @pl.loop(0, tasks)
    def _(task):
        basis = spread_basis(task)
        for part in range(shares):
            form_edges(task, basis, part, edges)
        contract(task, edges)

    energy = jnp.zeros((1, 1), jnp.float32)
    for number, place in enumerate(inside):
        alive = (
            lax.broadcasted_iota(jnp.int32, (slots, width), 0) < counts[0, index_of(place)]
        )
        rounded = [
            jnp.where(
                alive,
                near_state[part, pl.ds(starts[place], slots), :]
                + message_scale * fresh[number, part],
                0.0,
            ).astype(jnp.bfloat16)
            for part in range(4)
        ]
        if last:
            scalars_out[number] = rounded[0]
            for part in range(3):
                vectors_out[number, part] = rounded[part + 1]
            read = lax.dot_general(
                rounded[0],
                readout_in[...],
                (((1,), (1,)), ((), ())),
                preferred_element_type=jnp.float32,
            )
            read = read / (1.0 + jnp.exp(-read)) * readout_out[...]
            read = jnp.where(alive[:, : read.shape[1]], read, 0.0)
            energy = energy + jnp.sum(read, axis=(0, 1), keepdims=True)
        else:
            for part in range(4):
                block_out[number, part] = rounded[part]
    if last:
        spot = lax.broadcasted_iota(jnp.int32, part_out.shape, 1)
        part_out[...] = jnp.where(spot == 0, jnp.broadcast_to(energy, part_out.shape), 0.0)


def layer_update(layer, dims, basis_count, counts, tiles, near, params):
    wide, deep, tall = dims
    radial_out = params[1]
    around = math.prod(near.shape[:3])
    slots, width = near.shape[4:]
    hidden_width = radial_out.shape[1]
    last = layer == radial_out.shape[0] - 1
    cells = wide * deep * tall
    span = -(-around * slots // table_chunk) * table_chunk + chunk - table_chunk
    window = -(-(3 * (around // (wide + 2)) * slots + 16) // chunk) * chunk
    store = around * slots + window + slots
    vmem = pl.BlockSpec(memory_space=pltpu.VMEM)
    anywhere = pl.BlockSpec(memory_space=pl.ANY)
    if last:
        shapes = (
            jax.ShapeDtypeStruct((cells, slots, width), jnp.bfloat16),
            jax.ShapeDtypeStruct((cells, 3, slots, width), jnp.bfloat16),
            jax.ShapeDtypeStruct((1, 128), jnp.float32),
        )
    else:
        shapes = (jax.ShapeDtypeStruct((cells, 4, slots, width), jnp.bfloat16),)
    fetched = (counts, tiles, near) + params
    return pl.pallas_call(
        functools.partial(layer_kernel, dims, basis_count, layer, last),
        out_shape=shapes,
        in_specs=[anywhere] * len(fetched),
        out_specs=tuple(vmem for _ in shapes),
        scratch_shapes=[pltpu.SMEM(counts.shape, counts.dtype)]
        + [pltpu.VMEM(array.shape, array.dtype) for array in fetched[1:3]]
        + [pltpu.VMEM(array.shape[1:], array.dtype) for array in params[:4]]
        + [pltpu.VMEM(array.shape, array.dtype) for array in params[4:]]
        + [
            pltpu.VMEM((cells, 4, slots, width), jnp.float32),
            pltpu.VMEM((store, width), jnp.float32),
            pltpu.VMEM((cells, 5, slots, window), jnp.float32),
            pltpu.VMEM((4, store, width), jnp.float32),
            pltpu.VMEM((4, group * hidden_width, chunk), jnp.bfloat16),
            pltpu.VMEM((span, 4 * width), jnp.bfloat16),
            pltpu.VMEM((3, span, 2 * width), jnp.bfloat16),
            pltpu.SMEM((cells, 4), jnp.int32),
            pltpu.SMEM((cells * (slots // group) * (window // chunk), 3), jnp.int32),
            pltpu.SemaphoreType.DMA((wide + 2,)),
            pltpu.SemaphoreType.DMA((9,)),
        ],
        compiler_params=pltpu.CompilerParams(vmem_limit_bytes=56 << 20),
        name="message_layer",
    )(*fetched)


def on_device(
    positions,
    counts,
    scalars,
    vectors,
    radial_in,
    radial_bias,
    radial_out,
    atom_in,
    atom_bias,
    atom_out,
    readout_in,
    readout_out,
):
    dims = scalars.shape[:3]
    slots, width = scalars.shape[3:]
    level = counts.reshape(-1)
    rows = positions.reshape(-1, 1, slots)
    states = [
        scalars.transpose(2, 1, 0, 3, 4)[:, :, :, None],
        vectors.transpose(2, 1, 0, 4, 3, 5),
    ]
    params = (radial_out, atom_in, atom_out, atom_bias, readout_in.T, readout_out[None, :])
    near, tiles, near_counts, blocks = extended(
        states, dims, 0, (level, rows, radial_in, radial_bias)
    )
    params = (blocks,) + params
    layers = radial_in.shape[0]
    turned = dims[::-1]
    for layer in range(layers):
        made = layer_update(layer, dims, radial_in.shape[1], near_counts, tiles, near, params)
        if layer < layers - 1:
            (near,) = extended([made[0].reshape(turned + (4, slots, width))], dims, layer + 1)
    new_scalars, new_vectors, part = made
    scalar_state = new_scalars.reshape(turned + (slots, width)).transpose(2, 1, 0, 3, 4)
    vector_state = new_vectors.reshape(turned + (3, slots, width)).transpose(2, 1, 0, 4, 3, 5)
    energy = summed(part, ("gx", "gy", "gz"), layers)
    return (scalar_state, vector_state, energy)


def solution(mesh):
    block = P("gx", "gy", "gz")
    in_specs = (block,) * 4 + (P(),) * 8
    out_specs = (block, block, P())
    return jax.shard_map(
        on_device, mesh=mesh, in_specs=in_specs, out_specs=out_specs, check_vma=False
    )
```
